512 devices in a mesh: seq: 32 (over z, y_hi), doc: 16 (over x, y_lo, core).
Axes of the slice: x: 4, y: 8 (y_hi: 4, y_lo: 2; y = y_hi * 2 + y_lo), z: 8, core: 2. Of those that a mesh axis runs over, the one named last changes fastest.
Arguments:
- byte_q: bfloat16 [262144, 1024], P(('doc', 'seq')), parts along dimension 0, may hold values from -6 to 6
- byte_k: bfloat16 [262144, 1024], P(('doc', 'seq')), parts along dimension 0, may hold values from -6 to 6
- byte_v: bfloat16 [262144, 1024], P(('doc', 'seq')), parts along dimension 0, may hold values from -6 to 6
- byte_gain: bfloat16 [1024], replicated, may hold values from 0.2 to 4.5
- pool_query: bfloat16 [8, 128], replicated, may hold values from -12 to 12
- w_up: bfloat16 [1024, 2048], P('seq'), may hold values from -1 to 1
- patch_gain: bfloat16 [2048], replicated, may hold values from 0.099609375 to 1.8984375
- w_kv: bfloat16 [2048, 1024], P('seq'), may hold values from -1 to 1
- out_gain: bfloat16 [2048], replicated, may hold values from 0.2 to 4.5
- dec_gain: bfloat16 [1024], replicated, may hold values from 0.099609375 to 1.8984375
- patch_start: int32 [512, 80], P('doc'), parts along dimension 0, may hold values from 0 to 512, as said below
Outputs:
- byte_out: bfloat16 [262144, 1024], P(('doc', 'seq')), parts along dimension 0
- patch_out: bfloat16 [40960, 2048], P(('doc', 'seq')), parts along dimension 0
The draws below stay inside these ranges and needn't reach their ends.
There are 16 independent parts, one for each index of `doc`. The reference program is written for one: setup_inputs(seed, part) draws one part's arguments, and reference() takes and returns one part's arrays. A program takes and returns all parts, laid end to end along the dimension named above; an argument that names none is the same for every part. Nothing has to cross between parts.
Inputs may be any that keep to these rules, and one draw needn't show every extreme that they name: `patch_start`: row r lists the patch starts of block r: 0 first, strictly rising over its live slots, then 512 in every unused slot; each row has at least 20 live slots, and some row has all 80 live.
All inputs are finite; a program needn't handle non-finite values.
Results may differ from the reference program's by a relative error of at most 0.0085.
Values may be sent and summed in bfloat16 or wider, within the bound.
A program may use at most 128 MiB of HBM per device.

```python
import jax
import jax.numpy as jnp
from jax import lax

D = 1024
HB = 8
HD = 128
PATCH_WIDTH = 2048
PATCH_QUERY_HEADS = 32
PATCH_KEY_HEADS = 8
PATCH_HEAD_SIZE = 64
WINDOW = 512
BYTES_DEV = 512
PATCH_SLOTS = 80
LENGTH = 16384
N_SEQ = 32


def standard_gaussian(key, salt, shape, scale, bound):
    values = jax.random.normal(jax.random.fold_in(key, salt), shape, jnp.float32) * scale
    return jnp.clip(values, -bound, bound)


def draw_byte_q(key, part):
    return standard_gaussian(key, 23, (LENGTH, D), 1.0, 6.0).astype(jnp.bfloat16)


def draw_byte_k(key, part):
    return standard_gaussian(key, 24, (LENGTH, D), 1.0, 6.0).astype(jnp.bfloat16)


def draw_byte_v(key, part):
    return standard_gaussian(key, 25, (LENGTH, D), 1.0, 6.0).astype(jnp.bfloat16)


def draw_byte_gain(key, part):
    return (1.0 + 0.18 * standard_gaussian(key, 27, (D,), 1.0, 4.4)).astype(jnp.bfloat16)


def draw_out_gain(key, part):
    return (1.0 + 0.18 * standard_gaussian(key, 29, (PATCH_WIDTH,), 1.0, 4.4)).astype(jnp.bfloat16)


def draw_pool_query(key, part):
    return standard_gaussian(key, 31, (HB, HD), 2.0, 12.0).astype(jnp.bfloat16)


def draw_w_up(key, part):
    random_jitter = standard_gaussian(key, 32, (D, PATCH_WIDTH), 1.0, 4.0) * D ** (-0.5)
    return random_jitter.astype(jnp.bfloat16)


def draw_w_kv(key, part):
    random_jitter = standard_gaussian(key, 33, (PATCH_WIDTH, 2 * PATCH_KEY_HEADS * PATCH_HEAD_SIZE), 1.0, 4.0) * PATCH_WIDTH ** (-0.5)
    return random_jitter.astype(jnp.bfloat16)


def draw_patch_start(key, part):
    count_key = jax.random.fold_in(key, 11)
    full_key = jax.random.fold_in(key, 12)
    place_key = jax.random.fold_in(key, 13)
    counts = jax.random.randint(count_key, (N_SEQ,), PATCH_SLOTS // 4, PATCH_SLOTS + 1)
    full_row = jax.random.randint(full_key, (), 0, N_SEQ)
    counts = jnp.where(jnp.arange(N_SEQ) == full_row, PATCH_SLOTS, counts)
    row_keys = jax.random.split(place_key, N_SEQ)

    def one_row(row_key, live_count):
        shuffled = jax.random.permutation(row_key, BYTES_DEV - 1) + 1
        places = jnp.arange(BYTES_DEV - 1)
        chosen = jnp.where(places < live_count - 1, shuffled, BYTES_DEV)
        ordered = jnp.sort(chosen)[:PATCH_SLOTS - 1]
        return jnp.concatenate([jnp.zeros((1,), jnp.int32), ordered.astype(jnp.int32)])
    return jax.vmap(one_row)(row_keys, counts).astype(jnp.int32)


def setup_inputs(seed: int = 0, part: int = 0) -> dict:
    splits = jax.random.split(jax.random.key(seed), 12)
    part_splits = jax.random.split(jax.random.fold_in(splits[11], part), 12)
    byte_q = draw_byte_q(jax.random.fold_in(jax.random.fold_in(splits[11], part), 71), part)
    byte_k = draw_byte_k(jax.random.fold_in(jax.random.fold_in(splits[11], part), 71), part)
    byte_v = draw_byte_v(jax.random.fold_in(jax.random.fold_in(splits[11], part), 71), part)
    byte_gain = draw_byte_gain(jax.random.fold_in(splits[11], 71), part)
    pool_query = draw_pool_query(jax.random.fold_in(splits[11], 71), part)
    w_up = draw_w_up(jax.random.fold_in(splits[11], 71), part)
    patch_gain = jnp.clip(1.0 + 0.18 * jax.random.normal(splits[6], (PATCH_WIDTH,), jnp.float32), 0.099609375, 1.8984375).astype(jnp.bfloat16)
    w_kv = draw_w_kv(jax.random.fold_in(splits[11], 71), part)
    out_gain = draw_out_gain(jax.random.fold_in(splits[11], 71), part)
    dec_gain = jnp.clip(1.0 + 0.18 * jax.random.normal(splits[9], (D,), jnp.float32), 0.099609375, 1.8984375).astype(jnp.bfloat16)
    patch_start = draw_patch_start(jax.random.fold_in(jax.random.fold_in(splits[11], part), 71), part)
    return dict(byte_q=byte_q, byte_k=byte_k, byte_v=byte_v, byte_gain=byte_gain, pool_query=pool_query, w_up=w_up, patch_gain=patch_gain, w_kv=w_kv, out_gain=out_gain, dec_gain=dec_gain, patch_start=patch_start)


epsilon = 1e-06

def normed(matrix, gains):
    matrix = matrix.astype(jnp.float32)
    return matrix * lax.rsqrt(lax.optimization_barrier(jnp.mean(matrix * matrix, axis=-1, keepdims=True)) + epsilon) * gains.astype(jnp.float32)

def softmax_rows(scores, allowed):
    scores = jnp.where(allowed, scores, -jnp.inf)
    peak = lax.optimization_barrier(jnp.max(scores, axis=-1, keepdims=True))
    expo = jnp.where(allowed, jnp.exp(scores - peak), 0.0)
    return (expo / lax.optimization_barrier(jnp.sum(expo, axis=-1, keepdims=True))).astype(jnp.bfloat16)

def byte_block(query_rows, key_rows, value_rows, leading):
    nbytes = query_rows.shape[0]
    reach = key_rows.shape[0] - nbytes
    query_head_rows = query_rows.astype(jnp.float32).reshape(nbytes, HB, HD)
    key_head_rows = key_rows.astype(jnp.float32).reshape(nbytes + reach, HB, HD)
    value_head_rows = value_rows.astype(jnp.float32).reshape(nbytes + reach, HB, HD)
    scores = jnp.einsum('qhd,khd->hqk', query_head_rows, key_head_rows) * HD ** (-0.5)
    row_pos = jnp.arange(nbytes, dtype=jnp.int32)[:, None]
    col_pos = jnp.arange(nbytes + reach, dtype=jnp.int32)[None, :]
    allowed = (col_pos > row_pos) & (col_pos <= row_pos + reach) & ((col_pos >= reach) | jnp.logical_not(leading))
    weights = softmax_rows(scores, allowed[None])
    mixed = jnp.einsum('hqk,khd->qhd', weights.astype(jnp.float32), value_head_rows)
    return mixed.reshape(nbytes, HB * HD)

def segments(starts, nbytes):
    positions = jnp.arange(nbytes, dtype=jnp.int32)
    segment = (lax.optimization_barrier(jnp.sum((starts[None, :] <= positions[:, None]).astype(jnp.int32), axis=1)) - 1).astype(jnp.int32)
    member = segment[None, :] == jnp.arange(starts.shape[0], dtype=jnp.int32)[:, None]
    return (segment, member)

def pool(encoded, starts, pool_query):
    nbytes = encoded.shape[0]
    segment, member = segments(starts, nbytes)
    enc_heads = encoded.astype(jnp.float32).reshape(nbytes, HB, HD)
    scores = jnp.einsum('bhd,hd->bh', enc_heads, pool_query.astype(jnp.float32)) * HD ** (-0.5)
    inside = member[:, :, None]
    highest = lax.optimization_barrier(jnp.max(jnp.where(inside, scores[None], -jnp.inf), axis=1))
    own_max = lax.optimization_barrier(jnp.max(jnp.where(inside, highest[:, None, :], -jnp.inf), axis=0))
    expo = jnp.exp(scores - own_max)
    totals = lax.optimization_barrier(jnp.sum(jnp.where(inside, expo[None], 0.0), axis=1))
    divisor = lax.optimization_barrier(jnp.max(jnp.where(inside, totals[:, None, :], 0.0), axis=0))
    weights = (expo / divisor).astype(jnp.bfloat16)
    spread = jnp.where(inside, weights[None], jnp.zeros((), jnp.bfloat16))
    pooled = jnp.einsum('pbh,bhd->phd', spread.astype(jnp.float32), enc_heads)
    return pooled.reshape(starts.shape[0], HB * HD).astype(jnp.bfloat16)

def patch_block(query_rows, key_value_pairs, query_start, is_live):
    slot_total_count = query_rows.shape[0]
    overall_row_count = key_value_pairs.shape[0]
    head_groups = PATCH_QUERY_HEADS // PATCH_KEY_HEADS
    query_head_rows = query_rows.astype(jnp.float32).reshape(slot_total_count, PATCH_KEY_HEADS, head_groups, PATCH_HEAD_SIZE)
    key_head_rows = key_value_pairs[:, :PATCH_KEY_HEADS * PATCH_HEAD_SIZE].astype(jnp.float32).reshape(overall_row_count, PATCH_KEY_HEADS, PATCH_HEAD_SIZE)
    value_head_rows = key_value_pairs[:, PATCH_KEY_HEADS * PATCH_HEAD_SIZE:].astype(jnp.float32).reshape(overall_row_count, PATCH_KEY_HEADS, PATCH_HEAD_SIZE)
    scores = jnp.einsum('qkgd,pkd->kgqp', query_head_rows, key_head_rows) * PATCH_HEAD_SIZE ** (-0.5)
    query_pos = query_start + jnp.arange(slot_total_count, dtype=jnp.int32)
    key_pos = jnp.arange(overall_row_count, dtype=jnp.int32)
    allowed = (key_pos[None, :] <= query_pos[:, None]) & is_live[None, :]
    weights = softmax_rows(scores, allowed[None, None])
    mixed = jnp.einsum('kgqp,pkd->qkgd', weights.astype(jnp.float32), value_head_rows)
    return mixed.reshape(slot_total_count, PATCH_QUERY_HEADS * PATCH_HEAD_SIZE)

def decode(encoded, patch_rows, starts):
    nbytes = encoded.shape[0]
    slot_total_count = patch_rows.shape[0]
    segment, member = segments(starts, nbytes)
    enc_heads = encoded.astype(jnp.float32).reshape(nbytes, HB, HD)
    packed = patch_rows.astype(jnp.float32).reshape(slot_total_count, HB, 2, HD)
    scores = jnp.einsum('bhd,phd->hbp', enc_heads, packed[:, :, 0]) * HD ** (-0.5)
    allowed = jnp.arange(slot_total_count, dtype=jnp.int32)[None, :] <= segment[:, None]
    weights = softmax_rows(scores, allowed[None])
    mixed = jnp.einsum('hbp,phd->bhd', weights.astype(jnp.float32), packed[:, :, 1])
    return mixed.reshape(nbytes, HB * HD)

def reference(byte_q, byte_k, byte_v, byte_gain, pool_query, w_up, patch_gain, w_kv, out_gain, dec_gain, patch_start):
    reach = WINDOW
    nbytes = BYTES_DEV
    blank = jnp.zeros((reach, D), byte_k.dtype)
    key_padded = jnp.concatenate([blank, byte_k], axis=0)
    value_padded = jnp.concatenate([blank, byte_v], axis=0)

    def encode_one(device):
        query_rows = lax.dynamic_slice_in_dim(byte_q, device * nbytes, nbytes, 0)
        key_rows = lax.dynamic_slice_in_dim(key_padded, device * nbytes, reach + nbytes, 0)
        value_rows = lax.dynamic_slice_in_dim(value_padded, device * nbytes, reach + nbytes, 0)
        return normed(byte_block(query_rows, key_rows, value_rows, device == 0), byte_gain).astype(jnp.bfloat16)
    devices = jnp.arange(N_SEQ, dtype=jnp.int32)
    encoded = lax.map(encode_one, devices)
    pooled = lax.map(lambda operands: pool(operands[0], operands[1], pool_query), (encoded, patch_start))
    lifted = jnp.dot(pooled.reshape(N_SEQ * PATCH_SLOTS, D), w_up, preferred_element_type=jnp.float32)
    patch_input = normed(lifted, patch_gain).astype(jnp.bfloat16)
    key_value_pairs = jnp.dot(patch_input, w_kv, preferred_element_type=jnp.float32).astype(jnp.bfloat16)
    counts = lax.optimization_barrier(jnp.sum((patch_start < nbytes).astype(jnp.int32), axis=1))
    live_grid = jnp.arange(PATCH_SLOTS, dtype=jnp.int32)[None, :] < counts[:, None]
    is_live = live_grid.reshape(N_SEQ * PATCH_SLOTS)

    def attend_one(device):
        query_rows = lax.dynamic_slice_in_dim(patch_input, device * PATCH_SLOTS, PATCH_SLOTS, 0)
        mixed = patch_block(query_rows, key_value_pairs, device * PATCH_SLOTS, is_live)
        alive = lax.dynamic_index_in_dim(live_grid, device, 0, keepdims=False)
        return (normed(mixed, out_gain) * alive[:, None].astype(jnp.float32)).astype(jnp.bfloat16)
    patch_out = lax.map(attend_one, devices)

    def decode_one(operands):
        return normed(decode(operands[0], operands[1], operands[2]), dec_gain).astype(jnp.bfloat16)
    byte_out = lax.map(decode_one, (encoded, patch_out, patch_start))
    return (byte_out.reshape(N_SEQ * nbytes, D), patch_out.reshape(N_SEQ * PATCH_SLOTS, PATCH_QUERY_HEADS * PATCH_HEAD_SIZE))
```

```python
import functools

import jax
import jax.numpy as jnp
from jax import lax
from jax.experimental import pallas as pl
from jax.experimental.pallas import tpu as pltpu
from jax.sharding import PartitionSpec as P

EPS = 1e-06
LOG2E = 1.4426950408889634
BYTE_SCALE = 128 ** (-0.5) * LOG2E
PATCH_SCALE = 64 ** (-0.5) * LOG2E
NEG = -1e30
F32 = jnp.float32
BF16 = jnp.bfloat16
MESH = pl.DeviceIdType.MESH
NEAR_FIRST = (1, 7, 2, 6, 3, 5, 4)


def dot(a, b):
    return lax.dot_general(a, b, (((1,), (0,)), ((), ())), preferred_element_type=F32)


def dot_t(a, b):
    return lax.dot_general(a, b, (((1,), (1,)), ((), ())), preferred_element_type=F32)


def iota(shape, dim):
    return lax.broadcasted_iota(jnp.int32, shape, dim)


def as_row(column):
    return jnp.transpose(jnp.broadcast_to(column, (column.shape[0], 128)))[0:1]


def main_kernel(
    q_hbm, k_hbm, v_hbm, up_hbm, kv_hbm, byte_gain, pool_query, patch_gain, live_bias, starts,
    enc_hbm, mixed_hbm,
    q, k, v, q_next, o_send, o_recv, s_send, s_recv, o_own, s_own, enc, w, pooled, lifted, patch_in,
    x_q, x_kv, kv_all, q_all, o_out, o_in,
    load_sem, out_sem, q_ss, q_rs, o_ss, o_rs, s_ss, s_rs, wy_ss, wy_rs, wz_ss, wz_rs,
    wp_ss, wp_rs, wm_ss, wm_rs, w2_ss, w2_rs, wc_ss, wc_rs,
    kz_ss, kz_rs, qz_ss, qz_rs, yp_ss, yp_rs, ym_ss, ym_rs, yf_ss, yf_rs, oz_ss, oz_rs,
):
    s = lax.axis_index("seq")
    d = lax.axis_index("doc")
    z, yh = lax.div(s, 4), lax.rem(s, 4)
    x, rest, core = lax.div(d, 4), lax.rem(d, 4), lax.rem(d, 2)
    after, before = lax.rem(s + 1, 32), lax.rem(s + 31, 32)

    def along_y(step):
        return z * 4 + lax.rem(yh + step, 4)

    def along_z(step):
        return lax.rem(z + step, 8) * 4 + yh

    x_up, x_down = lax.rem(x + 1, 4) * 4 + rest, lax.rem(x + 3, 4) * 4 + rest
    partner = d + 1 - 2 * core

    def remote(src, dst, send, recv, seq, doc):
        return pltpu.make_async_remote_copy(
            src_ref=src, dst_ref=dst, send_sem=send, recv_sem=recv,
            device_id={"seq": seq, "doc": doc}, device_id_type=MESH,
        )

    def load(hbm, dst, which, h):
        cols = pl.ds(pl.multiple_of(h * 128, 128), 128)
        return pltpu.make_async_copy(hbm.at[:, cols], dst.at[h], load_sem.at[which, h])

    part = 2 * x + core

    def own_weights():
        ours = w.at[part, s]
        first = pl.multiple_of(part * 256, 256)
        return [
            pltpu.make_async_copy(up_hbm.at[:, pl.ds(first, 128)], ours.at[0:32], load_sem.at[3, 0]),
            pltpu.make_async_copy(up_hbm.at[:, pl.ds(first + 128, 128)], ours.at[32:64], load_sem.at[3, 1]),
            pltpu.make_async_copy(
                kv_hbm.at[:, pl.ds(pl.multiple_of(part * 128, 128), 128)], ours.at[64:128], load_sem.at[3, 2]
            ),
        ]

    @pl.loop(0, 8)
    def _(h):
        load(q_hbm, q, 0, h).start()

    for copy in own_weights():
        copy.start()

    @pl.loop(0, 8)
    def _(h):
        load(k_hbm, k, 1, h).start()
        load(v_hbm, v, 2, h).start()

    barrier = pltpu.get_barrier_semaphore()
    peers = [(after, d), (before, d), (s, x_up), (s, x_down), (s, partner)]
    peers += [(along_y(i), d) for i in (1, 2, 3)] + [(along_z(i), d) for i in NEAR_FIRST]
    for seq, doc in peers:
        pl.semaphore_signal(barrier, inc=1, device_id={"seq": seq, "doc": doc}, device_id_type=MESH)
    pl.semaphore_wait(barrier, len(peers))

    def send_query(h):
        return remote(q.at[h], q_next.at[h], q_ss.at[h], q_rs.at[h], before, d)

    @pl.loop(0, 8)
    def _(h):
        load(q_hbm, q, 0, h).wait()
        send_query(h).start()

    def block(p, step):
        return w.at[p, pl.ds(lax.rem(z + step, 8) * 4, 4)]

    def part_of(step):
        return 2 * lax.rem(x + step, 4) + core

    def w_y(step):
        ours = w.at[part, s]
        return remote(ours, ours, wy_ss.at[step - 1], wy_rs.at[step - 1], along_y(step), d)

    def w_y_arrival(step):
        slot = w.at[part, along_y(4 - step)]
        return remote(slot, slot, wy_ss.at[step - 1], wy_rs.at[step - 1], along_y(step), d)

    def w_z(step):
        ours = block(part, 0)
        return remote(ours, ours, wz_ss.at[step - 1], wz_rs.at[step - 1], along_z(step), d)

    def w_z_arrival(step):
        slot = block(part, 8 - step)
        return remote(slot, slot, wz_ss.at[step - 1], wz_rs.at[step - 1], along_z(step), d)

    def w_up(p, i):
        slot = block(p, i)
        return remote(slot, slot, wp_ss.at[i], wp_rs.at[i], s, x_up)

    def w_down(p, i):
        slot = block(p, i)
        return remote(slot, slot, wm_ss.at[i], wm_rs.at[i], s, x_down)

    def w_far(p, i):
        slot = block(p, i)
        return remote(slot, slot, w2_ss.at[i], w2_rs.at[i], s, x_up if i % 2 == 0 else x_down)

    def w_core(step, i, mine=True):
        p = part_of(step) if mine else 2 * lax.rem(x + step, 4) + 1 - core
        slot = block(p, i)
        return remote(slot, slot, wc_ss.at[step, i], wc_rs.at[step, i], s, partner)

    def spread(i):
        w_up(part, i).start()
        w_down(part, i).start()
        w_core(0, i).start()

    def from_x(i):
        w_up(part_of(3), i).wait_recv()
        if i % 2 == 0:
            w_far(part_of(3), i).start()
        w_core(3, i).start()
        w_down(part_of(1), i).wait_recv()
        if i % 2 == 1:
            w_far(part_of(1), i).start()
        w_core(1, i).start()

    def from_far(i):
        w_far(part_of(2), i).wait_recv()
        w_core(2, i).start()

    def weights_y():
        for copy in own_weights():
            copy.wait()
        for i in (1, 2, 3):
            w_y(i).start()

    def weights_z():
        for i in (1, 2, 3):
            w_y_arrival(i).wait_recv()
        for i in NEAR_FIRST:
            w_z(i).start()
        spread(0)

    def from_z(i):
        w_z_arrival(i).wait_recv()
        spread(8 - i)

    weights_y()

    def local_head(h):
        load(k_hbm, k, 1, h).wait()
        load(v_hbm, v, 2, h).wait()
        for half in (0, 1):
            rows, keys = pl.ds(256 * half, 256), 256 * (half + 1)
            t = dot_t(q[h, rows, :], k[h, 0:keys, :]) * BYTE_SCALE
            t = jnp.where(iota((256, keys), 1) <= iota((256, keys), 0) + 256 * half, t, NEG)
            peak = jnp.max(t, axis=1, keepdims=True)
            e = jnp.exp2(t - peak)
            total = jnp.sum(e, axis=1, keepdims=True)
            o_own[h, rows, :] = dot(e.astype(BF16), v[h, 0:keys, :]) * (1.0 / total)
            s_own[h, :, rows] = as_row(peak + jnp.log(total) * LOG2E)

    def remote_head(h):
        send_query(h).wait_recv()
        for half in (0, 1):
            rows, keys = pl.ds(256 * half, 256), 512 - 256 * half
            t = dot_t(q_next[h, rows, :], k[h, 256 * half : 512, :]) * BYTE_SCALE
            t = jnp.where(iota((256, keys), 1) > iota((256, keys), 0), t, NEG)
            peak = jnp.max(t, axis=1, keepdims=True)
            e = jnp.exp2(t - peak)
            total = jnp.sum(e, axis=1, keepdims=True)
            o = dot(e.astype(BF16), v[h, 256 * half : 512, :]) * (1.0 / total)
            o_send[h, rows, :] = o.astype(BF16)
            lse = peak + jnp.log(total) * LOG2E
            if half == 1:
                lse = jnp.where(iota((256, 1), 0) == 255, NEG, lse)
            s_send[h, :, rows] = as_row(lse)

    def send_out(h):
        return remote(o_send.at[h], o_recv.at[h], o_ss.at[h], o_rs.at[h], after, d)

    def send_stat(h):
        return remote(s_send.at[h], s_recv.at[h], s_ss.at[h], s_rs.at[h], after, d)

    @pl.loop(0, 8)
    def _(h):
        local_head(h)

        @pl.when(h == 1)
        def _():
            weights_z()

    stages = {
        0: [(from_z, 1), (from_z, 7)],
        1: [(from_z, 2), (from_z, 6), (from_x, 0)],
        2: [(from_z, 3), (from_z, 5), (from_x, 7), (from_x, 1), (from_far, 0)],
        3: [(from_z, 4), (from_x, 6), (from_x, 2), (from_far, 7), (from_far, 1)],
        4: [(from_x, 5), (from_x, 3), (from_far, 6), (from_far, 2)],
        5: [(from_x, 4), (from_far, 5), (from_far, 3)],
        6: [(from_far, 4)],
    }

    def forward(stage):
        for step, i in stage:
            step(i)

    @pl.loop(0, 8)
    def _(h):
        remote_head(h)
        send_out(h).start()
        send_stat(h).start()
        for at, stage in stages.items():
            pl.when(h == at)(functools.partial(forward, stage))

    def merge(h, squares):
        send_out(h).wait_recv()
        send_stat(h).wait_recv()
        own = s_own[h]
        other = jnp.where(s == 0, NEG, s_recv[h])
        peak = jnp.maximum(own, other)
        a, b = jnp.exp2(own - peak), jnp.exp2(other - peak)
        share = jnp.transpose(jnp.broadcast_to(b / (a + b), (128, 512)))
        mine = o_own[h]
        mix = mine + share * (o_recv[h].astype(F32) - mine)
        o_own[h] = mix
        return squares + mix * mix

    squares = lax.fori_loop(0, 8, merge, jnp.zeros((512, 128), F32))
    scale = lax.rsqrt(jnp.sum(squares, axis=1, keepdims=True) * (1.0 / 1024) + EPS)
    for h in range(8):
        enc[h] = (o_own[h] * scale * byte_gain[h : h + 1, :]).astype(BF16)
    enc_out = pltpu.make_async_copy(enc, enc_hbm, out_sem.at[0])
    enc_out.start()

    row = jnp.broadcast_to(starts[...].astype(F32), (80, 80))
    r80, c80 = iota((80, 80), 0), iota((80, 80), 1)
    first = jnp.sum(jnp.where(c80 == r80, row, 0.0), axis=1, keepdims=True)
    stop = jnp.sum(jnp.where(c80 == r80 + 1, row, 0.0), axis=1, keepdims=True)
    stop = jnp.where(iota((80, 1), 0) == 79, 512.0, stop)
    at = iota((80, 512), 1).astype(F32)
    member = (at >= first) & (at < stop)
    for h in range(8):
        score = dot_t(pool_query[...], enc[h])[h : h + 1, :] * BYTE_SCALE
        t = jnp.where(member, score, NEG)
        peak = jnp.max(t, axis=1, keepdims=True)
        e = jnp.where(member, jnp.exp2(t - peak), 0.0)
        total = jnp.sum(e, axis=1, keepdims=True)
        weights = (e / jnp.where(total > 0.0, total, 1.0)).astype(BF16)
        pooled[:, 128 * h : 128 * h + 128] = dot(weights, enc[h]).astype(BF16)

    for step in (0, 3, 1, 2):
        for i in (0, 7, 1, 6, 2, 5, 3, 4):
            w_core(step, i, mine=False).wait_recv()

    def lift(p, squares):
        left = w[p, :, 0:32, :].reshape(1024, 128)
        right = w[p, :, 32:64, :].reshape(1024, 128)
        got = dot(pooled[...], jnp.concatenate([left, right], axis=1))
        lifted[p] = got
        return squares + got * got

    squares = lax.fori_loop(0, 8, lift, jnp.zeros((80, 256), F32))
    scale = lax.rsqrt(jnp.sum(squares, axis=1, keepdims=True) * (1.0 / 2048) + EPS)
    for p in range(8):
        got = (lifted[p] * scale * patch_gain[p : p + 1, :]).astype(BF16)
        x_q[p] = got
        patch_in[:, 256 * p : 256 * p + 256] = got
    low = iota((80, 128), 1) < 64

    @pl.loop(0, 4)
    def _(p):
        keys = w[p, :, 64:128, :].reshape(2048, 128)
        values = w[p + 4, :, 64:128, :].reshape(2048, 128)
        got = dot(patch_in[...], jnp.concatenate([keys, values], axis=1))
        key, value = got[:, 0:128], got[:, 128:256]
        x_kv[2 * p] = jnp.where(low, key, pltpu.roll(value, 64, 1)).astype(BF16)
        x_kv[2 * p + 1] = jnp.where(low, pltpu.roll(key, 64, 1), value).astype(BF16)

    def kv_to(i):
        to = lax.rem(z + i, 8)
        return remote(x_kv.at[to], kv_all.at[z, yh], kz_ss.at[i - 1], kz_rs.at[i - 1], along_z(i), d)

    def q_to(i):
        to = lax.rem(z + i, 8)
        return remote(x_q.at[to], q_all.at[z], qz_ss.at[i - 1], qz_rs.at[i - 1], along_z(i), d)

    def kv_from(slot):
        i = lax.rem(z - slot + 7, 8)
        dst = kv_all.at[slot, yh]
        return remote(dst, dst, kz_ss.at[i], kz_rs.at[i], s, partner)

    def q_from(slot):
        i = lax.rem(z - slot + 7, 8)
        dst = q_all.at[slot]
        return remote(dst, dst, qz_ss.at[i], qz_rs.at[i], s, partner)

    for i in NEAR_FIRST:
        kv_to(i).start()
    for i in NEAR_FIRST:
        q_to(i).start()
    kv_all[z, yh] = x_kv[z]
    q_all[z] = x_q[z]

    y_up, y_down = lax.rem(yh + 1, 4), lax.rem(yh + 3, 4)

    def kv_up(slot, whose):
        ours = kv_all.at[slot, whose]
        return remote(ours, ours, yp_ss.at[slot], yp_rs.at[slot], along_y(1), d)

    def kv_down(slot, whose):
        ours = kv_all.at[slot, whose]
        return remote(ours, ours, ym_ss.at[slot], ym_rs.at[slot], along_y(3), d)

    def kv_far_up(slot, whose):
        ours = kv_all.at[slot, whose]
        return remote(ours, ours, yf_ss.at[slot], yf_rs.at[slot], along_y(1), d)

    def kv_far_down(slot, whose):
        ours = kv_all.at[slot, whose]
        return remote(ours, ours, yf_ss.at[slot], yf_rs.at[slot], along_y(3), d)

    @pl.loop(0, 8)
    def _(slot):
        @pl.when(slot != z)
        def _():
            kv_from(slot).wait_recv()

        kv_up(slot, yh).start()
        kv_down(slot, yh).start()

    def relay(slot):
        kv_up(slot, y_down).wait_recv()
        kv_down(slot, y_up).wait_recv()

        @pl.when(lax.rem(slot, 2) == 0)
        def _():
            kv_far_up(slot, y_down).start()

        @pl.when(lax.rem(slot, 2) == 1)
        def _():
            kv_far_down(slot, y_up).start()

    def out_to(to):
        return remote(o_out.at[to], o_in.at[z], oz_ss.at[to], oz_rs.at[z], to * 4 + yh, d)

    def out_from(slot):
        dst = o_in.at[slot]
        return remote(dst, dst, oz_ss.at[slot], oz_rs.at[slot], s, partner)

    r320 = iota((320, 1), 0)
    r320 = jnp.where(r320 >= 240, r320 - 240, jnp.where(r320 >= 160, r320 - 160, jnp.where(r320 >= 80, r320 - 80, r320)))

    def patch_block(slot):
        @pl.when(slot != z)
        def _():
            q_from(slot).wait_recv()

        heads = []
        for tile in (0, 1):
            pair = q_all[slot, :, 128 * tile : 128 * tile + 128].astype(F32)
            heads += [jnp.where(low, pair, 0.0), jnp.where(low, pltpu.roll(pair, 64, 1), 0.0)]
        query = jnp.concatenate(heads, axis=0).astype(BF16)
        query_pos = slot * 320 + yh * 80 + r320

        def chunk(c, state):
            peak, total, acc = state
            rows = kv_all[pl.ds(2 * c, 2)].reshape(640, 128)
            t = dot_t(query, rows) * PATCH_SCALE + live_bias[c]
            t = jnp.where(c * 640 + iota((320, 640), 1) <= query_pos, t, NEG)
            peak_new = jnp.maximum(peak, jnp.max(t, axis=1, keepdims=True))
            e = jnp.exp2(t - peak_new)
            fade = jnp.exp2(peak - peak_new)
            total = total * fade + jnp.sum(e, axis=1, keepdims=True)
            acc = acc * fade + dot(e.astype(BF16), rows)
            return peak_new, total, acc

        start = (jnp.full((320, 1), NEG, F32), jnp.zeros((320, 1), F32), jnp.zeros((320, 128), F32))
        _, total, acc = lax.fori_loop(0, lax.div(slot, 2) + 1, chunk, start)
        out = acc * (1.0 / total)
        for tile in (0, 1):
            even, odd = out[160 * tile : 160 * tile + 80], out[160 * tile + 80 : 160 * tile + 160]
            o_out[slot, :, 128 * tile : 128 * tile + 128] = jnp.where(low, pltpu.roll(even, 64, 1), odd).astype(BF16)

        @pl.when(slot != z)
        def _():
            out_to(slot).start()

        @pl.when(slot == z)
        def _():
            o_in[slot] = o_out[slot]

    def far_arrival(slot):
        kv_far_up(slot, lax.rem(yh + 2, 4)).wait_recv()

    for slot in (0, 1):
        relay(slot)
    far_arrival(0)

    @pl.loop(0, 8)
    def _(slot):
        @pl.when(slot < 6)
        def _():
            relay(slot + 2)

        @pl.when(slot < 7)
        def _():
            far_arrival(slot + 1)

        patch_block(slot)

    @pl.loop(0, 8)
    def _(slot):
        @pl.when(slot != z)
        def _():
            out_from(slot).wait_recv()

    mixed_out = pltpu.make_async_copy(o_in, mixed_hbm, out_sem.at[1])
    mixed_out.start()

    @pl.loop(0, 8)
    def _(h):
        send_query(h).wait_send()
        send_out(h).wait_send()
        send_stat(h).wait_send()
        kv_up(h, yh).wait_send()
        kv_down(h, yh).wait_send()
        kv_far_up(h, yh).wait_send()

        @pl.when(h != z)
        def _():
            out_to(h).wait_send()

    for i in (1, 2, 3):
        w_y(i).wait_send()
    for i in NEAR_FIRST:
        w_z(i).wait_send()
        kv_to(i).wait_send()
        q_to(i).wait_send()
    for i in range(8):
        w_up(part, i).wait_send()
        w_down(part, i).wait_send()
        w_far(part, i).wait_send()
        for step in range(4):
            w_core(step, i).wait_send()
    enc_out.wait()
    mixed_out.wait()


def decode_kernel(enc, mixed, out_gain, dec_gain, starts, byte_out, patch_out, cross):
    row = starts[...]
    wide = jnp.broadcast_to(row.astype(F32), (80, 80))
    first = jnp.sum(jnp.where(iota((80, 80), 1) == iota((80, 80), 0), wide, 0.0), axis=1, keepdims=True)
    alive = (first < 512.0).astype(F32)
    squares = jnp.zeros((80, 256), F32)
    for h in range(8):
        got = mixed[h].astype(F32)
        squares = squares + got * got
    scale = lax.rsqrt(jnp.sum(squares, axis=1, keepdims=True) * (1.0 / 2048) + EPS)
    allowed = row <= iota((512, 80), 0)
    squares = jnp.zeros((512, 128), F32)
    for h in range(8):
        patch = (mixed[h].astype(F32) * scale * out_gain[h : h + 1, :] * alive).astype(BF16)
        patch_out[:, 256 * h : 256 * h + 256] = patch
        t = jnp.where(allowed, dot_t(enc[h], patch[:, 0:128]) * BYTE_SCALE, NEG)
        peak = jnp.max(t, axis=1, keepdims=True)
        e = jnp.exp2(t - peak)
        total = jnp.sum(e, axis=1, keepdims=True)
        got = dot(e.astype(BF16), patch[:, 128:256]) * (1.0 / total)
        cross[h] = got
        squares = squares + got * got
    scale = lax.rsqrt(jnp.sum(squares, axis=1, keepdims=True) * (1.0 / 1024) + EPS)
    for h in range(8):
        byte_out[:, 128 * h : 128 * h + 128] = (cross[h] * scale * dec_gain[h : h + 1, :]).astype(BF16)


def per_device(
    byte_q, byte_k, byte_v, byte_gain, pool_query, w_up, patch_gain, w_kv, out_gain, dec_gain, patch_start
):
    starts = lax.dynamic_slice_in_dim(patch_start, lax.axis_index("seq"), 1, 0)
    live_bias = jnp.where(patch_start < 512, 0.0, NEG).astype(F32).reshape(4, 1, 640)
    hbm = pl.BlockSpec(memory_space=pl.ANY)
    vmem = pl.BlockSpec(memory_space=pltpu.VMEM)
    dma = pltpu.SemaphoreType.DMA
    enc, mixed = pl.pallas_call(
        main_kernel,
        out_shape=(
            jax.ShapeDtypeStruct((8, 512, 128), BF16),
            jax.ShapeDtypeStruct((8, 80, 256), BF16),
        ),
        in_specs=[hbm] * 5 + [vmem] * 5,
        out_specs=(hbm, hbm),
        scratch_shapes=[
            pltpu.VMEM((8, 512, 128), BF16),
            pltpu.VMEM((8, 512, 128), BF16),
            pltpu.VMEM((8, 512, 128), BF16),
            pltpu.VMEM((8, 512, 128), BF16),
            pltpu.VMEM((8, 512, 128), BF16),
            pltpu.VMEM((8, 512, 128), BF16),
            pltpu.VMEM((8, 1, 512), F32),
            pltpu.VMEM((8, 1, 512), F32),
            pltpu.VMEM((8, 512, 128), F32),
            pltpu.VMEM((8, 1, 512), F32),
            pltpu.VMEM((8, 512, 128), BF16),
            pltpu.VMEM((8, 32, 128, 128), BF16),
            pltpu.VMEM((80, 1024), BF16),
            pltpu.VMEM((8, 80, 256), F32),
            pltpu.VMEM((80, 2048), BF16),
            pltpu.VMEM((8, 80, 256), BF16),
            pltpu.VMEM((8, 80, 128), BF16),
            pltpu.VMEM((8, 4, 80, 128), BF16),
            pltpu.VMEM((8, 80, 256), BF16),
            pltpu.VMEM((8, 80, 256), BF16),
            pltpu.VMEM((8, 80, 256), BF16),
            dma((4, 8)),
            dma((2,)),
            *[dma((8,))] * 6,
            *[dma((3,))] * 2,
            *[dma((7,))] * 2,
            *[dma((8,))] * 6,
            *[dma((4, 8))] * 2,
            *[dma((7,))] * 4,
            *[dma((8,))] * 8,
        ],
        compiler_params=pltpu.CompilerParams(
            collective_id=0, has_side_effects=True, vmem_limit_bytes=60 * 1024 * 1024
        ),
    )(
        byte_q, byte_k, byte_v, w_up, w_kv,
        byte_gain.astype(F32).reshape(8, 128),
        jnp.concatenate([pool_query, pool_query], axis=0),
        patch_gain.astype(F32).reshape(8, 256),
        live_bias, starts,
    )
    return pl.pallas_call(
        decode_kernel,
        out_shape=(
            jax.ShapeDtypeStruct((512, 1024), BF16),
            jax.ShapeDtypeStruct((80, 2048), BF16),
        ),
        in_specs=[vmem] * 5,
        out_specs=(vmem, vmem),
        scratch_shapes=[pltpu.VMEM((8, 512, 128), F32)],
        compiler_params=pltpu.CompilerParams(vmem_limit_bytes=40 * 1024 * 1024),
    )(
        enc, mixed, out_gain.astype(F32).reshape(8, 256), dec_gain.astype(F32).reshape(8, 128), starts
    )


def solution(mesh):
    placed = (
        P(("doc", "seq"), None),
        P(("doc", "seq"), None),
        P(("doc", "seq"), None),
        P(),
        P(),
        P("seq", None),
        P(),
        P("seq", None),
        P(),
        P(),
        P("doc", None),
    )
    return jax.shard_map(
        per_device,
        mesh=mesh,
        in_specs=placed,
        out_specs=(P(("doc", "seq"), None), P(("doc", "seq"), None)),
        check_vma=False,
    )
```

```python
import functools

import jax
import jax.numpy as jnp
from jax import lax
from jax.experimental import pallas as pl
from jax.experimental.pallas import tpu as pltpu
from jax.sharding import PartitionSpec as P

EPS = 1e-06
LOG2E = 1.4426950408889634
BYTE_SCALE = 128 ** (-0.5) * LOG2E
PATCH_SCALE = 64 ** (-0.5) * LOG2E
NEG = -1e30
F32 = jnp.float32
BF16 = jnp.bfloat16
MESH = pl.DeviceIdType.MESH
IN_FLIGHT = 5
NEAR_FIRST = (1, 7, 2, 6, 3, 5, 4)


def dot(a, b):
    return lax.dot_general(a, b, (((1,), (0,)), ((), ())), preferred_element_type=F32)


def dot_t(a, b):
    return lax.dot_general(a, b, (((1,), (1,)), ((), ())), preferred_element_type=F32)


def iota(shape, dim):
    return lax.broadcasted_iota(jnp.int32, shape, dim)


def gain_row(ref, i, width):
    return ref[pl.ds(i * width, width)].astype(F32).reshape(1, width)


def as_row(column):
    return jnp.transpose(jnp.broadcast_to(column, (column.shape[0], 128)))[0:1]


def main_kernel(
    q_hbm, k_hbm, v_hbm, up_hbm, kv_hbm, byte_gain, pool_query, patch_gain, starts,
    enc_hbm, mixed_hbm,
    q, k, v, q_next, o_send, o_recv, s_send, s_recv, o_own, s_own, enc, w, pooled, lifted, patch_in,
    x_q, x_kv, kv_all, q_all, o_out, o_in, live_bias,
    load_sem, out_sem, q_ss, q_rs, o_ss, o_rs, s_ss, s_rs, wy_ss, wy_rs, zu_ss, zu_rs, zd_ss, zd_rs,
    wp_ss, wp_rs, wm_ss, wm_rs, w2_ss, w2_rs, wc_ss, wc_rs,
    kz_ss, kz_rs, qz_ss, qz_rs, yp_ss, yp_rs, ym_ss, ym_rs, yf_ss, yf_rs, oz_ss, oz_rs,
):
    s = lax.axis_index("seq")
    d = lax.axis_index("doc")
    z, yh = lax.div(s, 4), lax.rem(s, 4)
    x, rest, core = lax.div(d, 4), lax.rem(d, 4), lax.rem(d, 2)
    after, before = lax.rem(s + 1, 32), lax.rem(s + 31, 32)

    def along_y(step):
        return z * 4 + lax.rem(yh + step, 4)

    def along_z(step):
        return lax.rem(z + step, 8) * 4 + yh

    x_up, x_down = lax.rem(x + 1, 4) * 4 + rest, lax.rem(x + 3, 4) * 4 + rest
    partner = d + 1 - 2 * core

    def remote(src, dst, send, recv, seq, doc):
        return pltpu.make_async_remote_copy(
            src_ref=src, dst_ref=dst, send_sem=send, recv_sem=recv,
            device_id={"seq": seq, "doc": doc}, device_id_type=MESH,
        )

    def load(hbm, dst, which, h):
        cols = pl.ds(pl.multiple_of(h * 128, 128), 128)
        return pltpu.make_async_copy(hbm.at[:, cols], dst.at[h], load_sem.at[which])

    def loaded(dst, which):
        pltpu.make_async_copy(dst, dst, load_sem.at[which]).wait()

    def sent(ref, sem):
        remote(ref, ref, sem.at[0], sem.at[0], s, partner).wait_send()

    part = 2 * x + core

    def own_weights():
        ours = w.at[part, s]
        first = pl.multiple_of(part * 256, 256)
        return [
            pltpu.make_async_copy(up_hbm.at[:, pl.ds(first, 128)], ours.at[0:32], load_sem.at[3]),
            pltpu.make_async_copy(up_hbm.at[:, pl.ds(first + 128, 128)], ours.at[32:64], load_sem.at[3]),
            pltpu.make_async_copy(
                kv_hbm.at[:, pl.ds(pl.multiple_of(part * 128, 128), 128)], ours.at[64:128], load_sem.at[3]
            ),
        ]

    for copy in own_weights():
        copy.start()

    @pl.loop(0, 8)
    def _(h):
        load(q_hbm, q, 0, h).start()

    @pl.loop(0, 8)
    def _(h):
        load(k_hbm, k, 1, h).start()
        load(v_hbm, v, 2, h).start()

    barrier = pltpu.get_barrier_semaphore()
    peers = [(after, d), (before, d), (s, x_up), (s, x_down), (s, partner)]
    peers += [(along_y(i), d) for i in (1, 2, 3)] + [(along_z(i), d) for i in NEAR_FIRST]
    for seq, doc in peers:
        pl.semaphore_signal(barrier, inc=1, device_id={"seq": seq, "doc": doc}, device_id_type=MESH)
    pl.semaphore_wait(barrier, len(peers))

    def block(p, step):
        return w.at[p, pl.ds(lax.rem(z + step, 8) * 4, 4)]

    def part_of(step):
        return 2 * lax.rem(x + step, 4) + core

    def w_y(step):
        ours = w.at[part, s]
        return remote(ours, ours, wy_ss.at[0], wy_rs.at[0], along_y(step), d)

    def z_up(step):
        slot = block(part, (9 - step) % 8)
        return remote(slot, slot, zu_ss.at[0], zu_rs.at[step - 1], along_z(1), d)

    def z_down(step):
        slot = block(part, step - 1)
        return remote(slot, slot, zd_ss.at[0], zd_rs.at[step - 1], along_z(7), d)

    def w_up(p, i):
        slot = block(p, i)
        return remote(slot, slot, wp_ss.at[0], wp_rs.at[i], s, x_up)

    def w_down(p, i):
        slot = block(p, i)
        return remote(slot, slot, wm_ss.at[0], wm_rs.at[i], s, x_down)

    def w_far(p, i):
        slot = block(p, i)
        return remote(slot, slot, w2_ss.at[0], w2_rs.at[i], s, x_up if i % 2 == 0 else x_down)

    def w_core(step, i):
        slot = block(part_of(step), i)
        return remote(slot, slot, wc_ss.at[0], wc_rs.at[0], s, partner)

    def spread(i):
        w_up(part, i).start()
        w_down(part, i).start()
        w_core(0, i).start()

    def from_x(i):
        w_up(part_of(3), i).wait_recv()
        if i % 2 == 0:
            w_far(part_of(3), i).start()
        w_core(3, i).start()
        w_down(part_of(1), i).wait_recv()
        if i % 2 == 1:
            w_far(part_of(1), i).start()
        w_core(1, i).start()

    def from_far(i):
        w_far(part_of(2), i).wait_recv()
        w_core(2, i).start()

    def weights_y():
        loaded(w.at[part, s], 3)
        for i in (1, 2, 3):
            w_y(i).start()

    def weights_z():
        three = w.at[part, pl.ds(z * 4, 3)]
        remote(three, three, wy_ss.at[0], wy_rs.at[0], s, partner).wait_recv()
        z_up(1).start()
        z_down(1).start()
        spread(0)

    def from_z(step):
        z_up(step).wait_recv()
        if step < 4:
            z_up(step + 1).start()
            z_down(step).wait_recv()
        if step < 3:
            z_down(step + 1).start()
        spread(8 - step)
        if step < 4:
            spread(step)

    weights_y()

    def send_query(unit):
        h, half = lax.div(unit, 2), lax.rem(unit, 2)
        rows = pl.ds(pl.multiple_of(half * 256, 256), 256)
        return remote(q.at[h, rows], q_next.at[h, rows], q_ss.at[0], q_rs.at[unit], before, d)

    loaded(q, 0)
    for unit in range(IN_FLIGHT):
        send_query(unit).start()

    def local_head(h):
        for half in (0, 1):
            rows, keys = pl.ds(256 * half, 256), 256 * (half + 1)
            t = dot_t(q[h, rows, :], k[h, 0:keys, :]) * BYTE_SCALE
            t = jnp.where(iota((256, keys), 1) <= iota((256, keys), 0) + 256 * half, t, NEG)
            peak = jnp.max(t, axis=1, keepdims=True)
            e = jnp.exp2(t - peak)
            total = jnp.sum(e, axis=1, keepdims=True)
            o_own[h, rows, :] = dot(e.astype(BF16), v[h, 0:keys, :]) * (1.0 / total)
            s_own[h, :, rows] = as_row(peak + jnp.log(total) * LOG2E)

    def remote_half(h, half):
        rows, keys = pl.ds(256 * half, 256), 512 - 256 * half
        t = dot_t(q_next[h, rows, :], k[h, 256 * half : 512, :]) * BYTE_SCALE
        t = jnp.where(iota((256, keys), 1) > iota((256, keys), 0), t, NEG)
        peak = jnp.max(t, axis=1, keepdims=True)
        e = jnp.exp2(t - peak)
        total = jnp.sum(e, axis=1, keepdims=True)
        o = dot(e.astype(BF16), v[h, 256 * half : 512, :]) * (1.0 / total)
        o_send[h, rows, :] = o.astype(BF16)
        lse = peak + jnp.log(total) * LOG2E
        if half == 1:
            lse = jnp.where(iota((256, 1), 0) == 255, NEG, lse)
        s_send[h, :, rows] = as_row(lse)

    def send_out(h, half):
        rows = pl.ds(256 * half, 256)
        return remote(o_send.at[h, rows], o_recv.at[h, rows], o_ss.at[0], o_rs.at[h], after, d)

    def whole_out(h):
        return remote(o_send.at[h], o_recv.at[h], o_ss.at[0], o_rs.at[h], after, d)

    def send_stat(h):
        return remote(s_send.at[h], s_recv.at[h], s_ss.at[0], s_rs.at[h], after, d)

    local_stages = {4: [(weights_z,)]}
    stages = {
        0: [(from_z, 1)],
        2: [(from_z, 2)],
        4: [(from_z, 3), (from_x, 0)],
        6: [(from_z, 4), (from_x, 7)],
        7: [(from_x, 1)],
        8: [(from_x, 6), (from_far, 0)],
        10: [(from_x, 2), (from_far, 7)],
        11: [(from_x, 5), (from_far, 1)],
        12: [(from_x, 3), (from_far, 6)],
        13: [(from_x, 4), (from_far, 2)],
        14: [(from_far, 5)],
        15: [(from_far, 3), (from_far, 4)],
    }

    def forward(stage):
        for step, *i in stage:
            step(*i)

    loaded(k, 1)
    loaded(v, 2)

    @pl.loop(0, 8)
    def _(h):
        local_head(h)
        for at, stage in local_stages.items():
            pl.when(h == at)(functools.partial(forward, stage))

    p80, n80 = iota((80, 640), 0), iota((80, 640), 1)
    repeat = n80 == p80
    for i in range(1, 8):
        repeat = repeat | (n80 == p80 + 80 * i)
    of_row = iota((8, 640), 1) - 80 * iota((8, 640), 0)
    of_row = (of_row >= 0) & (of_row < 80)
    for c in range(4):
        live = (starts[8 * c : 8 * c + 8, :] < 512).astype(BF16)
        spread_out = dot(live, repeat.astype(BF16))
        live_bias[c] = jnp.sum(jnp.where(of_row, (spread_out - 1.0) * -NEG, 0.0), axis=0, keepdims=True)

    @pl.loop(0, 8)
    def _(h):
        for half in (0, 1):
            unit = 2 * h + half
            send_query(unit).wait_recv()

            @pl.when(unit < 16 - IN_FLIGHT)
            def _():
                send_query(unit + IN_FLIGHT).start()

            remote_half(h, half)
            send_out(h, half).start()
            if half == 1:
                send_stat(h).start()
            for at, stage in stages.items():
                if at % 2 == half:
                    pl.when(h == at // 2)(functools.partial(forward, stage))

    def merge(h, squares):
        whole_out(h).wait_recv()
        send_stat(h).wait_recv()
        own = s_own[h]
        other = jnp.where(s == 0, NEG, s_recv[h])
        peak = jnp.maximum(own, other)
        a, b = jnp.exp2(own - peak), jnp.exp2(other - peak)
        share = jnp.transpose(jnp.broadcast_to(b / (a + b), (128, 512)))
        mine = o_own[h]
        mix = mine + share * (o_recv[h].astype(F32) - mine)
        o_own[h] = mix
        return squares + mix * mix

    squares = lax.fori_loop(0, 8, merge, jnp.zeros((512, 128), F32))
    scale = lax.rsqrt(jnp.sum(squares, axis=1, keepdims=True) * (1.0 / 1024) + EPS)
    for h in range(8):
        enc[h] = (o_own[h] * scale * gain_row(byte_gain, h, 128)).astype(BF16)
    enc_out = pltpu.make_async_copy(enc, enc_hbm, out_sem.at[0])
    enc_out.start()

    row = jnp.broadcast_to(starts[pl.ds(s, 1), :].astype(F32), (80, 80))
    r80, c80 = iota((80, 80), 0), iota((80, 80), 1)
    first = jnp.sum(jnp.where(c80 == r80, row, 0.0), axis=1, keepdims=True)
    stop = jnp.sum(jnp.where(c80 == r80 + 1, row, 0.0), axis=1, keepdims=True)
    stop = jnp.where(iota((80, 1), 0) == 79, 512.0, stop)
    at = iota((80, 512), 1).astype(F32)
    member = (at >= first) & (at < stop)
    for h in range(8):
        score = dot_t(pool_query[...], enc[h])[h : h + 1, :] * BYTE_SCALE
        t = jnp.where(member, score, NEG)
        peak = jnp.max(t, axis=1, keepdims=True)
        e = jnp.where(member, jnp.exp2(t - peak), 0.0)
        total = jnp.sum(e, axis=1, keepdims=True)
        weights = (e / jnp.where(total > 0.0, total, 1.0)).astype(BF16)
        pooled[:, 128 * h : 128 * h + 128] = dot(weights, enc[h]).astype(BF16)

    half_of_w = w.at[0:4]
    remote(half_of_w, half_of_w, wc_ss.at[0], wc_rs.at[0], s, partner).wait_recv()

    def lift(p, squares):
        left = w[p, :, 0:32, :].reshape(1024, 128)
        right = w[p, :, 32:64, :].reshape(1024, 128)
        got = dot(pooled[...], jnp.concatenate([left, right], axis=1))
        lifted[p] = got
        return squares + got * got

    squares = lax.fori_loop(0, 8, lift, jnp.zeros((80, 256), F32))
    scale = lax.rsqrt(jnp.sum(squares, axis=1, keepdims=True) * (1.0 / 2048) + EPS)
    for p in range(8):
        got = (lifted[p] * scale * gain_row(patch_gain, p, 256)).astype(BF16)
        x_q[p] = got
        patch_in[:, 256 * p : 256 * p + 256] = got
    low = iota((80, 128), 1) < 64

    @pl.loop(0, 4)
    def _(p):
        keys = w[p, :, 64:128, :].reshape(2048, 128)
        values = w[p + 4, :, 64:128, :].reshape(2048, 128)
        got = dot(patch_in[...], jnp.concatenate([keys, values], axis=1))
        key, value = got[:, 0:128], got[:, 128:256]
        x_kv[2 * p] = jnp.where(low, key, pltpu.roll(value, 64, 1)).astype(BF16)
        x_kv[2 * p + 1] = jnp.where(low, pltpu.roll(key, 64, 1), value).astype(BF16)

    def kv_to(i):
        to = lax.rem(z + i, 8)
        return remote(x_kv.at[to], kv_all.at[z, yh], kz_ss.at[0], kz_rs.at[i - 1], along_z(i), d)

    def q_to(i):
        to = lax.rem(z + i, 8)
        return remote(x_q.at[to], q_all.at[z], qz_ss.at[0], qz_rs.at[i - 1], along_z(i), d)

    def kv_from(slot):
        i = lax.rem(z - slot + 7, 8)
        dst = kv_all.at[slot, yh]
        return remote(dst, dst, kz_ss.at[0], kz_rs.at[i], s, partner)

    def q_from(slot):
        i = lax.rem(z - slot + 7, 8)
        dst = q_all.at[slot]
        return remote(dst, dst, qz_ss.at[0], qz_rs.at[i], s, partner)

    for i in NEAR_FIRST:
        kv_to(i).start()
    for i in NEAR_FIRST:
        q_to(i).start()
    kv_all[z, yh] = x_kv[z]
    q_all[z] = x_q[z]

    sent(q, q_ss)
    sent(o_send, o_ss)
    sent(s_send, s_ss)
    sent(w.at[0, 0:3], wy_ss)
    sent(w.at[0, 0:16], zu_ss)
    sent(w.at[0, 0:12], zd_ss)
    sent(w.at[0], wp_ss)
    sent(w.at[0], wm_ss)
    sent(w.at[0], w2_ss)
    sent(half_of_w, wc_ss)

    y_up, y_down = lax.rem(yh + 1, 4), lax.rem(yh + 3, 4)

    def kv_up(slot, whose):
        ours = kv_all.at[slot, whose]
        return remote(ours, ours, yp_ss.at[0], yp_rs.at[slot], along_y(1), d)

    def kv_down(slot, whose):
        ours = kv_all.at[slot, whose]
        return remote(ours, ours, ym_ss.at[0], ym_rs.at[slot], along_y(3), d)

    def kv_far_up(slot, whose):
        ours = kv_all.at[slot, whose]
        return remote(ours, ours, yf_ss.at[0], yf_rs.at[slot], along_y(1), d)

    def kv_far_down(slot, whose):
        ours = kv_all.at[slot, whose]
        return remote(ours, ours, yf_ss.at[0], yf_rs.at[slot], along_y(3), d)

    def forward_kv(slot):
        @pl.when(slot != z)
        def _():
            kv_from(slot).wait_recv()

        kv_up(slot, yh).start()
        kv_down(slot, yh).start()

    def relay(slot):
        kv_up(slot, y_down).wait_recv()
        kv_down(slot, y_up).wait_recv()

        @pl.when(lax.rem(slot, 2) == 0)
        def _():
            kv_far_up(slot, y_down).start()

        @pl.when(lax.rem(slot, 2) == 1)
        def _():
            kv_far_down(slot, y_up).start()

    def out_to(to):
        return remote(o_out.at[to], o_in.at[z], oz_ss.at[0], oz_rs.at[z], to * 4 + yh, d)

    def out_from(slot):
        dst = o_in.at[slot]
        return remote(dst, dst, oz_ss.at[0], oz_rs.at[slot], s, partner)

    r320 = iota((320, 1), 0)
    r320 = jnp.where(r320 >= 240, r320 - 240, jnp.where(r320 >= 160, r320 - 160, jnp.where(r320 >= 80, r320 - 80, r320)))

    low_keys = iota((640, 128), 1) < 64

    def gathered_query(slot):
        @pl.when(slot != z)
        def _():
            q_from(slot).wait_recv()

        heads = []
        for tile in (0, 1):
            pair = q_all[slot, :, 128 * tile : 128 * tile + 128].astype(F32)
            heads += [jnp.where(low, pair, 0.0), jnp.where(low, pltpu.roll(pair, 64, 1), 0.0)]
        return jnp.concatenate(heads, axis=0).astype(BF16)

    def patch_pair(pair):
        slots = (2 * pair, 2 * pair + 1)
        queries = [gathered_query(slot) for slot in slots]

        def chunk(c, state, last):
            rows = kv_all[pl.ds(2 * c, 2)].reshape(640, 128)
            values = jnp.where(low_keys, jnp.ones((), BF16), rows)
            bias = live_bias[c]
            new = []
            for i in (0, 1):
                peak, acc = state[i]
                t = dot_t(queries[i], rows) * PATCH_SCALE + bias
                if last:
                    t = jnp.where(iota((320, 640), 1) <= i * 320 + yh * 80 + r320, t, NEG)
                peak_new = jnp.maximum(peak, jnp.max(t, axis=1, keepdims=True))
                e = jnp.exp2(t - peak_new).astype(BF16)
                new.append((peak_new, acc * jnp.exp2(peak - peak_new) + dot(e, values)))
            return tuple(new)

        start = (jnp.full((320, 1), NEG, F32), jnp.zeros((320, 128), F32))
        state = lax.fori_loop(0, pair, functools.partial(chunk, last=False), (start, start))
        state = chunk(pair, state, True)
        for slot, (_, acc) in zip(slots, state):
            out = acc * (1.0 / acc[:, 0:1])
            for tile in (0, 1):
                even, odd = out[160 * tile : 160 * tile + 80], out[160 * tile + 80 : 160 * tile + 160]
                o_out[slot, :, 128 * tile : 128 * tile + 128] = jnp.where(low, pltpu.roll(even, 64, 1), odd).astype(BF16)

            @pl.when(slot != z)
            def _():
                out_to(slot).start()

            @pl.when(slot == z)
            def _():
                o_in[slot] = o_out[slot]

    def far_arrival(slot):
        kv_far_up(slot, lax.rem(yh + 2, 4)).wait_recv()

    @pl.loop(0, 4)
    def _(slot):
        forward_kv(slot)

    @pl.loop(0, 4)
    def _(pair):
        @pl.when(pair == 0)
        def _():
            relay(0)
            relay(1)
            forward_kv(4)
            forward_kv(5)

        @pl.when(pair == 1)
        def _():
            forward_kv(6)
            forward_kv(7)

        @pl.when(pair < 3)
        def _():
            relay(2 * pair + 2)
            relay(2 * pair + 3)

        far_arrival(2 * pair)
        far_arrival(2 * pair + 1)
        patch_pair(pair)

    def mixed_out(slot):
        return pltpu.make_async_copy(o_in.at[slot], mixed_hbm.at[slot], out_sem.at[1])

    @pl.loop(0, 8)
    def _(slot):
        @pl.when(slot != z)
        def _():
            out_from(slot).wait_recv()

        mixed_out(slot).start()

    sent(x_kv.at[0:7], kz_ss)
    sent(x_q.at[0:7], qz_ss)
    sent(x_kv, yp_ss)
    sent(x_kv, ym_ss)
    sent(x_kv, yf_ss)
    sent(o_out.at[0:7], oz_ss)
    enc_out.wait()
    pltpu.make_async_copy(o_in, mixed_hbm, out_sem.at[1]).wait()


def decode_kernel(enc_hbm, mixed_hbm, out_gain, dec_gain, starts, byte_out, patch_out, cross, enc, mixed, sem, enc_sem):
    mixed_in = pltpu.make_async_copy(mixed_hbm, mixed, sem)
    mixed_in.start()

    enc_in = pltpu.make_async_copy(enc_hbm, enc, enc_sem)
    enc_in.start()
    row = starts[pl.ds(lax.axis_index("seq"), 1), :]
    wide = jnp.broadcast_to(row.astype(F32), (80, 80))
    first = jnp.sum(jnp.where(iota((80, 80), 1) == iota((80, 80), 0), wide, 0.0), axis=1, keepdims=True)
    alive = (first < 512.0).astype(F32)
    mixed_in.wait()
    enc_in.wait()
    squares = jnp.zeros((80, 256), F32)
    for h in range(8):
        got = mixed[h].astype(F32)
        squares = squares + got * got
    scale = lax.rsqrt(jnp.sum(squares, axis=1, keepdims=True) * (1.0 / 2048) + EPS)
    allowed = row <= iota((512, 80), 0)
    squares = jnp.zeros((512, 128), F32)
    for h in range(8):
        patch = (mixed[h].astype(F32) * scale * gain_row(out_gain, h, 256) * alive).astype(BF16)
        patch_out[:, 256 * h : 256 * h + 256] = patch
        t = jnp.where(allowed, dot_t(enc[h], patch[:, 0:128]) * BYTE_SCALE, NEG)
        peak = jnp.max(t, axis=1, keepdims=True)
        e = jnp.exp2(t - peak)
        total = jnp.sum(e, axis=1, keepdims=True)
        got = dot(e.astype(BF16), patch[:, 128:256]) * (1.0 / total)
        cross[h] = got
        squares = squares + got * got
    scale = lax.rsqrt(jnp.sum(squares, axis=1, keepdims=True) * (1.0 / 1024) + EPS)
    for h in range(8):
        byte_out[:, 128 * h : 128 * h + 128] = (cross[h] * scale * gain_row(dec_gain, h, 128)).astype(BF16)


def per_device(
    byte_q, byte_k, byte_v, byte_gain, pool_query, w_up, patch_gain, w_kv, out_gain, dec_gain, patch_start
):
    hbm = pl.BlockSpec(memory_space=pl.ANY)
    vmem = pl.BlockSpec(memory_space=pltpu.VMEM)
    dma = pltpu.SemaphoreType.DMA
    enc, mixed = pl.pallas_call(
        main_kernel,
        out_shape=(
            jax.ShapeDtypeStruct((8, 512, 128), BF16),
            jax.ShapeDtypeStruct((8, 80, 256), BF16),
        ),
        in_specs=[hbm] * 5 + [vmem] * 4,
        out_specs=(hbm, hbm),
        scratch_shapes=[
            pltpu.VMEM((8, 512, 128), BF16),
            pltpu.VMEM((8, 512, 128), BF16),
            pltpu.VMEM((8, 512, 128), BF16),
            pltpu.VMEM((8, 512, 128), BF16),
            pltpu.VMEM((8, 512, 128), BF16),
            pltpu.VMEM((8, 512, 128), BF16),
            pltpu.VMEM((8, 1, 512), F32),
            pltpu.VMEM((8, 1, 512), F32),
            pltpu.VMEM((8, 512, 128), F32),
            pltpu.VMEM((8, 1, 512), F32),
            pltpu.VMEM((8, 512, 128), BF16),
            pltpu.VMEM((8, 32, 128, 128), BF16),
            pltpu.VMEM((80, 1024), BF16),
            pltpu.VMEM((8, 80, 256), F32),
            pltpu.VMEM((80, 2048), BF16),
            pltpu.VMEM((8, 80, 256), BF16),
            pltpu.VMEM((8, 80, 128), BF16),
            pltpu.VMEM((8, 4, 80, 128), BF16),
            pltpu.VMEM((8, 80, 256), BF16),
            pltpu.VMEM((8, 80, 256), BF16),
            pltpu.VMEM((8, 80, 256), BF16),
            pltpu.VMEM((4, 1, 640), F32),
            dma((4,)),
            dma((2,)),
            *[dma((1,)), dma((16,))],
            *[dma((1,)), dma((8,))] * 2,
            *[dma((1,)), dma((1,))],
            *[dma((1,)), dma((4,))],
            *[dma((1,)), dma((3,))],
            *[dma((1,)), dma((8,))] * 3,
            *[dma((1,)), dma((1,))],
            *[dma((1,)), dma((7,))] * 2,
            *[dma((1,)), dma((8,))] * 4,
        ],
        compiler_params=pltpu.CompilerParams(
            collective_id=0, has_side_effects=True, vmem_limit_bytes=60 * 1024 * 1024
        ),
    )(
        byte_q, byte_k, byte_v, w_up, w_kv,
        byte_gain, pool_query, patch_gain, patch_start,
    )
    return pl.pallas_call(
        decode_kernel,
        out_shape=(
            jax.ShapeDtypeStruct((512, 1024), BF16),
            jax.ShapeDtypeStruct((80, 2048), BF16),
        ),
        in_specs=[hbm] * 2 + [vmem] * 3,
        out_specs=(vmem, vmem),
        scratch_shapes=[
            pltpu.VMEM((8, 512, 128), F32),
            pltpu.VMEM((8, 512, 128), BF16),
            pltpu.VMEM((8, 80, 256), BF16),
            dma,
            dma,
        ],
        compiler_params=pltpu.CompilerParams(vmem_limit_bytes=60 * 1024 * 1024),
    )(
        enc, mixed, out_gain, dec_gain, patch_start
    )


def solution(mesh):
    placed = (
        P(("doc", "seq"), None),
        P(("doc", "seq"), None),
        P(("doc", "seq"), None),
        P(),
        P(),
        P("seq", None),
        P(),
        P("seq", None),
        P(),
        P(),
        P("doc", None),
    )
    return jax.shard_map(
        per_device,
        mesh=mesh,
        in_specs=placed,
        out_specs=(P(("doc", "seq"), None), P(("doc", "seq"), None)),
        check_vma=False,
    )
```

```python
import functools

import jax
import jax.numpy as jnp
from jax import lax
from jax.experimental import pallas as pl
from jax.experimental.pallas import tpu as pltpu
from jax.sharding import PartitionSpec as P

EPS = 1e-06
LOG2E = 1.4426950408889634
BYTE_SCALE = 128 ** (-0.5) * LOG2E
PATCH_SCALE = 64 ** (-0.5) * LOG2E
NEG = -1e30
F32 = jnp.float32
BF16 = jnp.bfloat16
MESH = pl.DeviceIdType.MESH
IN_FLIGHT = 4
FAR_FIRST = (4, 3, 5, 2, 6, 1, 7)


def dot(a, b):
    return lax.dot_general(a, b, (((1,), (0,)), ((), ())), preferred_element_type=F32)


def dot_t(a, b):
    return lax.dot_general(a, b, (((1,), (1,)), ((), ())), preferred_element_type=F32)


def iota(shape, dim):
    return lax.broadcasted_iota(jnp.int32, shape, dim)


def gain_row(ref, i, width):
    return ref[pl.ds(i * width, width)].astype(F32).reshape(1, width)


def as_row(column):
    return jnp.transpose(jnp.broadcast_to(column, (column.shape[0], 128)))[0:1]


def main_kernel(
    q_hbm, k_hbm, v_hbm, up_hbm, kv_hbm, byte_gain, pool_query, patch_gain, starts,
    enc_hbm, mixed_hbm,
    q, k, v, q_next, k_prev, v_prev, o_send, o_recv, s_send, s_recv, o_own, s_own, enc, w, pooled, lifted, patch_in,
    x_q, x_kv, kv_all, q_all, o_out, o_in, live_bias,
    load_sem, out_sem, kp_ss, kp_rs, q_ss, q_rs, o_ss, o_rs, s_ss, s_rs, wy_ss, wy_rs, zu_ss, zu_rs, zd_ss, zd_rs,
    wp_ss, wp_rs, wm_ss, wm_rs, w2_ss, w2_rs, wc_ss, wc_rs,
    kz_ss, kz_rs, qz_ss, qz_rs, yp_ss, yp_rs, ym_ss, ym_rs, yf_ss, yf_rs, oz_ss, oz_rs,
):
    s = lax.axis_index("seq")
    d = lax.axis_index("doc")
    z, yh = lax.div(s, 4), lax.rem(s, 4)
    x, rest, core = lax.div(d, 4), lax.rem(d, 4), lax.rem(d, 2)
    after, before = lax.rem(s + 1, 32), lax.rem(s + 31, 32)

    def along_y(step):
        return z * 4 + lax.rem(yh + step, 4)

    def along_z(step):
        return lax.rem(z + step, 8) * 4 + yh

    x_up, x_down = lax.rem(x + 1, 4) * 4 + rest, lax.rem(x + 3, 4) * 4 + rest
    partner = d + 1 - 2 * core

    def remote(src, dst, send, recv, seq, doc):
        return pltpu.make_async_remote_copy(
            src_ref=src, dst_ref=dst, send_sem=send, recv_sem=recv,
            device_id={"seq": seq, "doc": doc}, device_id_type=MESH,
        )

    def load(hbm, dst, which, h):
        cols = pl.ds(pl.multiple_of(h * 128, 128), 128)
        return pltpu.make_async_copy(hbm.at[:, cols], dst.at[h], load_sem.at[which])

    def loaded(dst, which):
        pltpu.make_async_copy(dst, dst, load_sem.at[which]).wait()

    def sent(ref, sem):
        remote(ref, ref, sem.at[0], sem.at[0], s, partner).wait_send()

    part = 2 * x + core

    def own_weights():
        ours = w.at[part, s]
        first = pl.multiple_of(part * 256, 256)
        return [
            pltpu.make_async_copy(up_hbm.at[:, pl.ds(first, 128)], ours.at[0:32], load_sem.at[3]),
            pltpu.make_async_copy(up_hbm.at[:, pl.ds(first + 128, 128)], ours.at[32:64], load_sem.at[3]),
            pltpu.make_async_copy(
                kv_hbm.at[:, pl.ds(pl.multiple_of(part * 128, 128), 128)], ours.at[64:128], load_sem.at[3]
            ),
        ]

    for copy in own_weights():
        copy.start()

    @pl.loop(0, 8)
    def _(h):
        load(q_hbm, q, 0, h).start()

    @pl.loop(0, 8)
    def _(h):
        load(k_hbm, k, 1, h).start()
        load(v_hbm, v, 2, h).start()

    barrier = pltpu.get_barrier_semaphore()
    peers = [(after, d), (before, d), (s, x_up), (s, x_down), (s, partner)]
    peers += [(along_y(i), d) for i in (1, 2, 3)] + [(along_z(i), d) for i in FAR_FIRST]
    for seq, doc in peers:
        pl.semaphore_signal(barrier, inc=1, device_id={"seq": seq, "doc": doc}, device_id_type=MESH)
    pl.semaphore_wait(barrier, len(peers))

    def block(p, step):
        return w.at[p, pl.ds(lax.rem(z + step, 8) * 4, 4)]

    def part_of(step):
        return 2 * lax.rem(x + step, 4) + core

    def w_y(step):
        ours = w.at[part, s]
        return remote(ours, ours, wy_ss.at[0], wy_rs.at[0], along_y(step), d)

    def z_up(step):
        slot = block(part, (9 - step) % 8)
        return remote(slot, slot, zu_ss.at[0], zu_rs.at[step - 1], along_z(1), d)

    def z_down(step):
        slot = block(part, step - 1)
        return remote(slot, slot, zd_ss.at[0], zd_rs.at[step - 1], along_z(7), d)

    def w_up(p, i):
        slot = block(p, i)
        return remote(slot, slot, wp_ss.at[0], wp_rs.at[i], s, x_up)

    def w_down(p, i):
        slot = block(p, i)
        return remote(slot, slot, wm_ss.at[0], wm_rs.at[i], s, x_down)

    def w_far(p, i):
        slot = block(p, i)
        return remote(slot, slot, w2_ss.at[0], w2_rs.at[i], s, x_up if i % 2 == 0 else x_down)

    def w_core(step, i):
        slot = block(part_of(step), i)
        return remote(slot, slot, wc_ss.at[0], wc_rs.at[0], s, partner)

    def spread(i):
        w_up(part, i).start()
        w_down(part, i).start()
        w_core(0, i).start()

    def from_x(i):
        w_up(part_of(3), i).wait_recv()
        if i % 2 == 0:
            w_far(part_of(3), i).start()
        w_core(3, i).start()
        w_down(part_of(1), i).wait_recv()
        if i % 2 == 1:
            w_far(part_of(1), i).start()
        w_core(1, i).start()

    def from_far(i):
        w_far(part_of(2), i).wait_recv()
        w_core(2, i).start()

    def weights_y():
        loaded(w.at[part, s], 3)
        for i in (1, 2, 3):
            w_y(i).start()

    def weights_z():
        three = w.at[part, pl.ds(z * 4, 3)]
        remote(three, three, wy_ss.at[0], wy_rs.at[0], s, partner).wait_recv()
        z_up(1).start()
        z_down(1).start()
        spread(0)

    def from_z(step):
        z_up(step).wait_recv()
        if step < 4:
            z_up(step + 1).start()
            z_down(step).wait_recv()
        if step < 3:
            z_down(step + 1).start()
        spread(8 - step)
        if step < 4:
            spread(step)

    weights_y()

    def send_query(unit):
        h, half = lax.div(unit, 2), lax.rem(unit, 2)
        rows = pl.ds(pl.multiple_of(half * 256, 256), 256)
        return remote(q.at[h, rows], q_next.at[h, rows], q_ss.at[0], q_rs.at[unit], before, d)

    def send_keys(which):
        own, dst = ((k, k_prev), (v, v_prev))[which]
        return remote(own.at[7], dst, kp_ss.at[which], kp_rs.at[which], after, d)

    loaded(q, 0)
    send_query(0).start()
    loaded(k, 1)
    loaded(v, 2)
    send_keys(0).start()
    send_keys(1).start()

    def local_head(h):
        for half in (0, 1):
            rows, keys = pl.ds(256 * half, 256), 256 * (half + 1)
            t = dot_t(q[h, rows, :], k[h, 0:keys, :]) * BYTE_SCALE
            t = jnp.where(iota((256, keys), 1) <= iota((256, keys), 0) + 256 * half, t, NEG)
            peak = jnp.max(t, axis=1, keepdims=True)
            e = jnp.exp2(t - peak)
            total = jnp.sum(e, axis=1, keepdims=True)
            o_own[h, rows, :] = dot(e.astype(BF16), v[h, 0:keys, :]) * (1.0 / total)
            s_own[h, :, rows] = as_row(peak + jnp.log(total) * LOG2E)

    def cross_half(half, queries, keys, values, o_dst, s_dst):
        rows, n = pl.ds(256 * half, 256), 512 - 256 * half
        t = dot_t(queries[rows, :], keys[256 * half : 512, :]) * BYTE_SCALE
        t = jnp.where(iota((256, n), 1) > iota((256, n), 0), t, NEG)
        peak = jnp.max(t, axis=1, keepdims=True)
        e = jnp.exp2(t - peak)
        total = jnp.sum(e, axis=1, keepdims=True)
        o = dot(e.astype(BF16), values[256 * half : 512, :]) * (1.0 / total)
        o_dst[rows, :] = o.astype(BF16)
        lse = peak + jnp.log(total) * LOG2E
        if half == 1:
            lse = jnp.where(iota((256, 1), 0) == 255, NEG, lse)
        s_dst[:, rows] = as_row(lse)

    def remote_half(h, half):
        cross_half(half, q_next.at[h], k.at[h], v.at[h], o_send.at[h], s_send.at[h])

    def last_head():
        send_keys(0).wait_recv()
        send_keys(1).wait_recv()
        for half in (0, 1):
            cross_half(half, q.at[7], k_prev, v_prev, o_recv.at[7], s_recv.at[7])

    def send_out(h, half):
        rows = pl.ds(256 * half, 256)
        return remote(o_send.at[h, rows], o_recv.at[h, rows], o_ss.at[0], o_rs.at[h], after, d)

    def whole_out(h):
        return remote(o_send.at[h], o_recv.at[h], o_ss.at[0], o_rs.at[h], after, d)

    def send_stat(h):
        return remote(s_send.at[h], s_recv.at[h], s_ss.at[0], s_rs.at[h], after, d)

    stages = {
        0: [(from_z, 1)],
        1: [(from_x, 0)],
        2: [(from_z, 2)],
        4: [(from_z, 3), (from_x, 7)],
        5: [(from_x, 1)],
        6: [(from_z, 4), (from_far, 0)],
        7: [(from_x, 6), (last_head,)],
        8: [(from_x, 2)],
        9: [(from_far, 7)],
        10: [(from_x, 5), (from_far, 1)],
        11: [(from_x, 3), (from_x, 4)],
        12: [(from_far, 6)],
        13: [(from_far, 2)],
    }

    def forward(stage):
        for step, *i in stage:
            step(*i)

    @pl.loop(0, 4)
    def _(h):
        local_head(h)

        @pl.when(h < 3)
        def _():
            send_query(h + 1).start()

    weights_z()

    p80, n80 = iota((80, 640), 0), iota((80, 640), 1)
    repeat = n80 == p80
    for i in range(1, 8):
        repeat = repeat | (n80 == p80 + 80 * i)
    of_row = iota((8, 640), 1) - 80 * iota((8, 640), 0)
    of_row = (of_row >= 0) & (of_row < 80)
    for c in range(4):
        live = (starts[8 * c : 8 * c + 8, :] < 512).astype(BF16)
        spread_out = dot(live, repeat.astype(BF16))
        live_bias[c] = jnp.sum(jnp.where(of_row, (spread_out - 1.0) * -NEG, 0.0), axis=0, keepdims=True)

    @pl.loop(0, 7)
    def _(h):
        for half in (0, 1):
            unit = 2 * h + half
            send_query(unit).wait_recv()

            @pl.when(unit < 14 - IN_FLIGHT)
            def _():
                send_query(unit + IN_FLIGHT).start()

            remote_half(h, half)
            send_out(h, half).start()
            if half == 1:
                send_stat(h).start()

            @pl.when(h < 2)
            def _():
                local_head(4 + unit)

            for at, stage in stages.items():
                if at % 2 == half:
                    pl.when(h == at // 2)(functools.partial(forward, stage))

    for i in (5, 3, 4):
        from_far(i)

    def merge(h, squares):
        @pl.when(h < 7)
        def _():
            whole_out(h).wait_recv()
            send_stat(h).wait_recv()

        own = s_own[h]
        other = jnp.where(s == 0, NEG, s_recv[h])
        peak = jnp.maximum(own, other)
        a, b = jnp.exp2(own - peak), jnp.exp2(other - peak)
        share = jnp.transpose(jnp.broadcast_to(b / (a + b), (128, 512)))
        mine = o_own[h]
        mix = mine + share * (o_recv[h].astype(F32) - mine)
        o_own[h] = mix
        return squares + mix * mix

    squares = lax.fori_loop(0, 8, merge, jnp.zeros((512, 128), F32))
    scale = lax.rsqrt(jnp.sum(squares, axis=1, keepdims=True) * (1.0 / 1024) + EPS)
    for h in range(8):
        enc[h] = (o_own[h] * scale * gain_row(byte_gain, h, 128)).astype(BF16)
    enc_out = pltpu.make_async_copy(enc, enc_hbm, out_sem.at[0])
    enc_out.start()

    row = jnp.broadcast_to(starts[pl.ds(s, 1), :].astype(F32), (80, 80))
    r80, c80 = iota((80, 80), 0), iota((80, 80), 1)
    first = jnp.sum(jnp.where(c80 == r80, row, 0.0), axis=1, keepdims=True)
    stop = jnp.sum(jnp.where(c80 == r80 + 1, row, 0.0), axis=1, keepdims=True)
    stop = jnp.where(iota((80, 1), 0) == 79, 512.0, stop)
    at = iota((80, 512), 1).astype(F32)
    member = (at >= first) & (at < stop)
    for h in range(8):
        score = dot_t(pool_query[...], enc[h])[h : h + 1, :] * BYTE_SCALE
        t = jnp.where(member, score, NEG)
        peak = jnp.max(t, axis=1, keepdims=True)
        e = jnp.where(member, jnp.exp2(t - peak), 0.0)
        total = jnp.sum(e, axis=1, keepdims=True)
        weights = (e / jnp.where(total > 0.0, total, 1.0)).astype(BF16)
        pooled[:, 128 * h : 128 * h + 128] = dot(weights, enc[h]).astype(BF16)

    half_of_w = w.at[0:4]
    remote(half_of_w, half_of_w, wc_ss.at[0], wc_rs.at[0], s, partner).wait_recv()

    def lift(p, squares):
        left = w[p, :, 0:32, :].reshape(1024, 128)
        right = w[p, :, 32:64, :].reshape(1024, 128)
        got = dot(pooled[...], jnp.concatenate([left, right], axis=1))
        lifted[p] = got
        return squares + got * got

    squares = lax.fori_loop(0, 8, lift, jnp.zeros((80, 256), F32))
    scale = lax.rsqrt(jnp.sum(squares, axis=1, keepdims=True) * (1.0 / 2048) + EPS)
    for p in range(8):
        got = (lifted[p] * scale * gain_row(patch_gain, p, 256)).astype(BF16)
        x_q[p] = got
        patch_in[:, 256 * p : 256 * p + 256] = got
    low = iota((80, 128), 1) < 64

    @pl.loop(0, 4)
    def _(p):
        keys = w[p, :, 64:128, :].reshape(2048, 128)
        values = w[p + 4, :, 64:128, :].reshape(2048, 128)
        got = dot(patch_in[...], jnp.concatenate([keys, values], axis=1))
        key, value = got[:, 0:128], got[:, 128:256]
        x_kv[2 * p] = jnp.where(low, key, pltpu.roll(value, 64, 1)).astype(BF16)
        x_kv[2 * p + 1] = jnp.where(low, pltpu.roll(key, 64, 1), value).astype(BF16)

    def kv_to(i):
        to = lax.rem(z + i, 8)
        return remote(x_kv.at[to], kv_all.at[z, yh], kz_ss.at[0], kz_rs.at[i - 1], along_z(i), d)

    def q_to(i):
        to = lax.rem(z + i, 8)
        return remote(x_q.at[to], q_all.at[z], qz_ss.at[0], qz_rs.at[i - 1], along_z(i), d)

    def kv_from(slot):
        i = lax.rem(z - slot + 7, 8)
        dst = kv_all.at[slot, yh]
        return remote(dst, dst, kz_ss.at[0], kz_rs.at[i], s, partner)

    def q_from(slot):
        i = lax.rem(z - slot + 7, 8)
        dst = q_all.at[slot]
        return remote(dst, dst, qz_ss.at[0], qz_rs.at[i], s, partner)

    for i in FAR_FIRST:
        kv_to(i).start()
    for i in FAR_FIRST:
        q_to(i).start()
    kv_all[z, yh] = x_kv[z]
    q_all[z] = x_q[z]

    sent(q.at[0:7], q_ss)
    sent(o_send.at[0:7], o_ss)
    sent(s_send.at[0:7], s_ss)
    send_keys(0).wait_send()
    send_keys(1).wait_send()
    sent(w.at[0, 0:3], wy_ss)
    sent(w.at[0, 0:16], zu_ss)
    sent(w.at[0, 0:12], zd_ss)
    sent(w.at[0], wp_ss)
    sent(w.at[0], wm_ss)
    sent(w.at[0], w2_ss)
    sent(half_of_w, wc_ss)

    y_up, y_down = lax.rem(yh + 1, 4), lax.rem(yh + 3, 4)

    def kv_up(slot, whose):
        ours = kv_all.at[slot, whose]
        return remote(ours, ours, yp_ss.at[0], yp_rs.at[slot], along_y(1), d)

    def kv_down(slot, whose):
        ours = kv_all.at[slot, whose]
        return remote(ours, ours, ym_ss.at[0], ym_rs.at[slot], along_y(3), d)

    def kv_far_up(slot, whose):
        ours = kv_all.at[slot, whose]
        return remote(ours, ours, yf_ss.at[0], yf_rs.at[slot], along_y(1), d)

    def kv_far_down(slot, whose):
        ours = kv_all.at[slot, whose]
        return remote(ours, ours, yf_ss.at[0], yf_rs.at[slot], along_y(3), d)

    def forward_kv(slot):
        @pl.when(slot != z)
        def _():
            kv_from(slot).wait_recv()

        kv_up(slot, yh).start()
        kv_down(slot, yh).start()

    def relay(slot):
        kv_up(slot, y_down).wait_recv()
        kv_down(slot, y_up).wait_recv()

        @pl.when(lax.rem(slot, 2) == 0)
        def _():
            kv_far_up(slot, y_down).start()

        @pl.when(lax.rem(slot, 2) == 1)
        def _():
            kv_far_down(slot, y_up).start()

    def out_to(to):
        return remote(o_out.at[to], o_in.at[z], oz_ss.at[0], oz_rs.at[z], to * 4 + yh, d)

    def out_from(slot):
        dst = o_in.at[slot]
        return remote(dst, dst, oz_ss.at[0], oz_rs.at[slot], s, partner)

    r320 = iota((320, 1), 0)
    r320 = jnp.where(r320 >= 240, r320 - 240, jnp.where(r320 >= 160, r320 - 160, jnp.where(r320 >= 80, r320 - 80, r320)))

    low_keys = iota((640, 128), 1) < 64

    def gathered_query(slot):
        @pl.when(slot != z)
        def _():
            q_from(slot).wait_recv()

        heads = []
        for tile in (0, 1):
            pair = q_all[slot, :, 128 * tile : 128 * tile + 128].astype(F32)
            heads += [jnp.where(low, pair, 0.0), jnp.where(low, pltpu.roll(pair, 64, 1), 0.0)]
        return jnp.concatenate(heads, axis=0).astype(BF16)

    def patch_pair(pair):
        slots = (2 * pair, 2 * pair + 1)
        queries = [gathered_query(slot) for slot in slots]

        def chunk(c, state, last):
            rows = kv_all[pl.ds(2 * c, 2)].reshape(640, 128)
            values = jnp.where(low_keys, jnp.ones((), BF16), rows)
            bias = live_bias[c]
            new = []
            for i in (0, 1):
                peak, acc = state[i]
                t = dot_t(queries[i], rows) * PATCH_SCALE + bias
                if last:
                    t = jnp.where(iota((320, 640), 1) <= i * 320 + yh * 80 + r320, t, NEG)
                peak_new = jnp.maximum(peak, jnp.max(t, axis=1, keepdims=True))
                e = jnp.exp2(t - peak_new).astype(BF16)
                new.append((peak_new, acc * jnp.exp2(peak - peak_new) + dot(e, values)))
            return tuple(new)

        start = (jnp.full((320, 1), NEG, F32), jnp.zeros((320, 128), F32))
        state = lax.fori_loop(0, pair, functools.partial(chunk, last=False), (start, start))
        state = chunk(pair, state, True)
        for slot, (_, acc) in zip(slots, state):
            out = acc * (1.0 / acc[:, 0:1])
            for tile in (0, 1):
                even, odd = out[160 * tile : 160 * tile + 80], out[160 * tile + 80 : 160 * tile + 160]
                o_out[slot, :, 128 * tile : 128 * tile + 128] = jnp.where(low, pltpu.roll(even, 64, 1), odd).astype(BF16)

            @pl.when(slot != z)
            def _():
                out_to(slot).start()

            @pl.when(slot == z)
            def _():
                o_in[slot] = o_out[slot]

    def far_arrival(slot):
        kv_far_up(slot, lax.rem(yh + 2, 4)).wait_recv()

    @pl.loop(0, 4)
    def _(slot):
        forward_kv(slot)

    @pl.loop(0, 4)
    def _(pair):
        @pl.when(pair == 0)
        def _():
            relay(0)
            relay(1)
            forward_kv(4)
            forward_kv(5)

        @pl.when(pair == 1)
        def _():
            forward_kv(6)
            forward_kv(7)

        @pl.when(pair < 3)
        def _():
            relay(2 * pair + 2)
            relay(2 * pair + 3)

        far_arrival(2 * pair)
        far_arrival(2 * pair + 1)
        patch_pair(pair)

    def mixed_out(slot):
        return pltpu.make_async_copy(o_in.at[slot], mixed_hbm.at[slot], out_sem.at[1])

    @pl.loop(0, 8)
    def _(slot):
        @pl.when(slot != z)
        def _():
            out_from(slot).wait_recv()

        mixed_out(slot).start()

    sent(x_kv.at[0:7], kz_ss)
    sent(x_q.at[0:7], qz_ss)
    sent(x_kv, yp_ss)
    sent(x_kv, ym_ss)
    sent(x_kv, yf_ss)
    sent(o_out.at[0:7], oz_ss)
    enc_out.wait()
    pltpu.make_async_copy(o_in, mixed_hbm, out_sem.at[1]).wait()


def decode_kernel(enc_hbm, mixed_hbm, out_gain, dec_gain, starts, byte_out, patch_out, cross, enc, mixed, sem, enc_sem):
    mixed_in = pltpu.make_async_copy(mixed_hbm, mixed, sem)
    mixed_in.start()

    enc_in = pltpu.make_async_copy(enc_hbm, enc, enc_sem)
    enc_in.start()
    row = starts[pl.ds(lax.axis_index("seq"), 1), :]
    wide = jnp.broadcast_to(row.astype(F32), (80, 80))
    first = jnp.sum(jnp.where(iota((80, 80), 1) == iota((80, 80), 0), wide, 0.0), axis=1, keepdims=True)
    alive = (first < 512.0).astype(F32)
    mixed_in.wait()
    enc_in.wait()
    squares = jnp.zeros((80, 256), F32)
    for h in range(8):
        got = mixed[h].astype(F32)
        squares = squares + got * got
    scale = lax.rsqrt(jnp.sum(squares, axis=1, keepdims=True) * (1.0 / 2048) + EPS)
    allowed = row <= iota((512, 80), 0)
    squares = jnp.zeros((512, 128), F32)
    for h in range(8):
        patch = (mixed[h].astype(F32) * scale * gain_row(out_gain, h, 256) * alive).astype(BF16)
        patch_out[:, 256 * h : 256 * h + 256] = patch
        t = jnp.where(allowed, dot_t(enc[h], patch[:, 0:128]) * BYTE_SCALE, NEG)
        peak = jnp.max(t, axis=1, keepdims=True)
        e = jnp.exp2(t - peak)
        total = jnp.sum(e, axis=1, keepdims=True)
        got = dot(e.astype(BF16), patch[:, 128:256]) * (1.0 / total)
        cross[h] = got
        squares = squares + got * got
    scale = lax.rsqrt(jnp.sum(squares, axis=1, keepdims=True) * (1.0 / 1024) + EPS)
    for h in range(8):
        byte_out[:, 128 * h : 128 * h + 128] = (cross[h] * scale * gain_row(dec_gain, h, 128)).astype(BF16)


def per_device(
    byte_q, byte_k, byte_v, byte_gain, pool_query, w_up, patch_gain, w_kv, out_gain, dec_gain, patch_start
):
    hbm = pl.BlockSpec(memory_space=pl.ANY)
    vmem = pl.BlockSpec(memory_space=pltpu.VMEM)
    dma = pltpu.SemaphoreType.DMA
    enc, mixed = pl.pallas_call(
        main_kernel,
        out_shape=(
            jax.ShapeDtypeStruct((8, 512, 128), BF16),
            jax.ShapeDtypeStruct((8, 80, 256), BF16),
        ),
        in_specs=[hbm] * 5 + [vmem] * 4,
        out_specs=(hbm, hbm),
        scratch_shapes=[
            pltpu.VMEM((8, 512, 128), BF16),
            pltpu.VMEM((8, 512, 128), BF16),
            pltpu.VMEM((8, 512, 128), BF16),
            pltpu.VMEM((8, 512, 128), BF16),
            pltpu.VMEM((512, 128), BF16),
            pltpu.VMEM((512, 128), BF16),
            pltpu.VMEM((8, 512, 128), BF16),
            pltpu.VMEM((8, 512, 128), BF16),
            pltpu.VMEM((8, 1, 512), F32),
            pltpu.VMEM((8, 1, 512), F32),
            pltpu.VMEM((8, 512, 128), F32),
            pltpu.VMEM((8, 1, 512), F32),
            pltpu.VMEM((8, 512, 128), BF16),
            pltpu.VMEM((8, 32, 128, 128), BF16),
            pltpu.VMEM((80, 1024), BF16),
            pltpu.VMEM((8, 80, 256), F32),
            pltpu.VMEM((80, 2048), BF16),
            pltpu.VMEM((8, 80, 256), BF16),
            pltpu.VMEM((8, 80, 128), BF16),
            pltpu.VMEM((8, 4, 80, 128), BF16),
            pltpu.VMEM((8, 80, 256), BF16),
            pltpu.VMEM((8, 80, 256), BF16),
            pltpu.VMEM((8, 80, 256), BF16),
            pltpu.VMEM((4, 1, 640), F32),
            dma((4,)),
            dma((2,)),
            dma((2,)),
            dma((2,)),
            *[dma((1,)), dma((16,))],
            *[dma((1,)), dma((8,))] * 2,
            *[dma((1,)), dma((1,))],
            *[dma((1,)), dma((4,))],
            *[dma((1,)), dma((3,))],
            *[dma((1,)), dma((8,))] * 3,
            *[dma((1,)), dma((1,))],
            *[dma((1,)), dma((7,))] * 2,
            *[dma((1,)), dma((8,))] * 4,
        ],
        compiler_params=pltpu.CompilerParams(
            collective_id=0, has_side_effects=True, vmem_limit_bytes=60 * 1024 * 1024
        ),
    )(
        byte_q, byte_k, byte_v, w_up, w_kv,
        byte_gain, pool_query, patch_gain, patch_start,
    )
    return pl.pallas_call(
        decode_kernel,
        out_shape=(
            jax.ShapeDtypeStruct((512, 1024), BF16),
            jax.ShapeDtypeStruct((80, 2048), BF16),
        ),
        in_specs=[hbm] * 2 + [vmem] * 3,
        out_specs=(vmem, vmem),
        scratch_shapes=[
            pltpu.VMEM((8, 512, 128), F32),
            pltpu.VMEM((8, 512, 128), BF16),
            pltpu.VMEM((8, 80, 256), BF16),
            dma,
            dma,
        ],
        compiler_params=pltpu.CompilerParams(vmem_limit_bytes=60 * 1024 * 1024),
    )(
        enc, mixed, out_gain, dec_gain, patch_start
    )


def solution(mesh):
    placed = (
        P(("doc", "seq"), None),
        P(("doc", "seq"), None),
        P(("doc", "seq"), None),
        P(),
        P(),
        P("seq", None),
        P(),
        P("seq", None),
        P(),
        P(),
        P("doc", None),
    )
    return jax.shard_map(
        per_device,
        mesh=mesh,
        in_specs=placed,
        out_specs=(P(("doc", "seq"), None), P(("doc", "seq"), None)),
        check_vma=False,
    )
```

```python
import functools

import jax
import jax.numpy as jnp
from jax import lax
from jax.experimental import pallas as pl
from jax.experimental.pallas import tpu as pltpu
from jax.sharding import PartitionSpec as P

EPS = 1e-06
LOG2E = 1.4426950408889634
BYTE_SCALE = 128 ** (-0.5) * LOG2E
PATCH_SCALE = 64 ** (-0.5) * LOG2E
NEG = -1e30
F32 = jnp.float32
BF16 = jnp.bfloat16
MESH = pl.DeviceIdType.MESH
IN_FLIGHT = 4
FAR_FIRST = (4, 3, 5, 2, 6, 1, 7)


def dot(a, b):
    return lax.dot_general(a, b, (((1,), (0,)), ((), ())), preferred_element_type=F32)


def dot_t(a, b):
    return lax.dot_general(a, b, (((1,), (1,)), ((), ())), preferred_element_type=F32)


def iota(shape, dim):
    return lax.broadcasted_iota(jnp.int32, shape, dim)


def gain_row(ref, i, width):
    return ref[pl.ds(i * width, width)].astype(F32).reshape(1, width)


def as_row(column):
    return jnp.transpose(jnp.broadcast_to(column, (column.shape[0], 128)))[0:1]


def main_kernel(
    q_hbm, k_hbm, v_hbm, up_hbm, kv_hbm, byte_gain, pool_query, patch_gain, starts,
    enc_hbm, mixed_hbm,
    q, k, v, q_next, k_prev, v_prev, o_send, o_recv, s_send, s_recv, o_own, s_own, enc, w, pooled, lifted, patch_in,
    x_q, x_kv, kv_all, q_all, o_out, o_in, live_bias,
    load_sem, out_sem, kp_ss, kp_rs, q_ss, q_rs, o_ss, o_rs, s_ss, s_rs, wy_ss, wy_rs, zu_ss, zu_rs, zd_ss, zd_rs,
    wp_ss, wp_rs, wm_ss, wm_rs, w2_ss, w2_rs, wc_ss, wc_rs,
    kz_ss, kz_rs, qz_ss, qz_rs, yp_ss, yp_rs, ym_ss, ym_rs, yf_ss, yf_rs, oz_ss, oz_rs,
):
    s = lax.axis_index("seq")
    d = lax.axis_index("doc")
    z, yh = lax.div(s, 4), lax.rem(s, 4)
    x, rest, core = lax.div(d, 4), lax.rem(d, 4), lax.rem(d, 2)
    after, before = lax.rem(s + 1, 32), lax.rem(s + 31, 32)

    def along_y(step):
        return z * 4 + lax.rem(yh + step, 4)

    def along_z(step):
        return lax.rem(z + step, 8) * 4 + yh

    x_up, x_down = lax.rem(x + 1, 4) * 4 + rest, lax.rem(x + 3, 4) * 4 + rest
    partner = d + 1 - 2 * core

    def remote(src, dst, send, recv, seq, doc):
        return pltpu.make_async_remote_copy(
            src_ref=src, dst_ref=dst, send_sem=send, recv_sem=recv,
            device_id={"seq": seq, "doc": doc}, device_id_type=MESH,
        )

    def load(hbm, dst, which, h):
        cols = pl.ds(pl.multiple_of(h * 128, 128), 128)
        return pltpu.make_async_copy(hbm.at[:, cols], dst.at[h], load_sem.at[which])

    def loaded(dst, which):
        pltpu.make_async_copy(dst, dst, load_sem.at[which]).wait()

    def sent(ref, sem):
        remote(ref, ref, sem.at[0], sem.at[0], s, partner).wait_send()

    part = 2 * x + core

    def own_weights():
        ours = w.at[part, s]
        first = pl.multiple_of(part * 256, 256)
        return [
            pltpu.make_async_copy(up_hbm.at[:, pl.ds(first, 128)], ours.at[0:32], load_sem.at[3]),
            pltpu.make_async_copy(up_hbm.at[:, pl.ds(first + 128, 128)], ours.at[32:64], load_sem.at[3]),
            pltpu.make_async_copy(
                kv_hbm.at[:, pl.ds(pl.multiple_of(part * 128, 128), 128)], ours.at[64:128], load_sem.at[3]
            ),
        ]

    for copy in own_weights():
        copy.start()

    @pl.loop(0, 8)
    def _(h):
        load(q_hbm, q, 0, h).start()

    @pl.loop(0, 8)
    def _(h):
        load(k_hbm, k, 1, h).start()
        load(v_hbm, v, 2, h).start()

    barrier = pltpu.get_barrier_semaphore()
    peers = [(after, d), (before, d), (s, x_up), (s, x_down), (s, partner)]
    peers += [(along_y(i), d) for i in (1, 2, 3)] + [(along_z(i), d) for i in FAR_FIRST]
    for seq, doc in peers:
        pl.semaphore_signal(barrier, inc=1, device_id={"seq": seq, "doc": doc}, device_id_type=MESH)
    pl.semaphore_wait(barrier, len(peers))

    def block(p, step):
        return w.at[p, pl.ds(lax.rem(z + step, 8) * 4, 4)]

    def part_of(step):
        return 2 * lax.rem(x + step, 4) + core

    def w_y(step):
        ours = w.at[part, s]
        return remote(ours, ours, wy_ss.at[0], wy_rs.at[0], along_y(step), d)

    def z_up(step):
        slot = block(part, (9 - step) % 8)
        return remote(slot, slot, zu_ss.at[0], zu_rs.at[step - 1], along_z(1), d)

    def z_down(step):
        slot = block(part, step - 1)
        return remote(slot, slot, zd_ss.at[0], zd_rs.at[step - 1], along_z(7), d)

    def w_up(p, i):
        slot = block(p, i)
        return remote(slot, slot, wp_ss.at[0], wp_rs.at[i], s, x_up)

    def w_down(p, i):
        slot = block(p, i)
        return remote(slot, slot, wm_ss.at[0], wm_rs.at[i], s, x_down)

    def w_far(p, i):
        slot = block(p, i)
        return remote(slot, slot, w2_ss.at[0], w2_rs.at[i], s, x_up if i % 2 == 0 else x_down)

    def w_core(step, i):
        slot = block(part_of(step), i)
        return remote(slot, slot, wc_ss.at[0], wc_rs.at[0], s, partner)

    def spread(i):
        w_up(part, i).start()
        w_down(part, i).start()
        w_core(0, i).start()

    def from_x(i):
        w_up(part_of(3), i).wait_recv()
        if i % 2 == 0:
            w_far(part_of(3), i).start()
        w_core(3, i).start()
        w_down(part_of(1), i).wait_recv()
        if i % 2 == 1:
            w_far(part_of(1), i).start()
        w_core(1, i).start()

    def from_far(i):
        w_far(part_of(2), i).wait_recv()
        w_core(2, i).start()

    def weights_y():
        loaded(w.at[part, s], 3)
        for i in (1, 2, 3):
            w_y(i).start()

    def weights_z():
        three = w.at[part, pl.ds(z * 4, 3)]
        remote(three, three, wy_ss.at[0], wy_rs.at[0], s, partner).wait_recv()
        z_up(1).start()
        z_down(1).start()
        spread(0)

    def from_z(step):
        z_up(step).wait_recv()
        if step < 4:
            z_up(step + 1).start()
            z_down(step).wait_recv()
        if step < 3:
            z_down(step + 1).start()
        spread(8 - step)
        if step < 4:
            spread(step)

    weights_y()

    def send_query(unit):
        h, half = lax.div(unit, 2), lax.rem(unit, 2)
        rows = pl.ds(pl.multiple_of(half * 256, 256), 256)
        return remote(q.at[h, rows], q_next.at[h, rows], q_ss.at[0], q_rs.at[unit], before, d)

    def send_keys(which):
        own, dst = ((k, k_prev), (v, v_prev))[which]
        return remote(own.at[7], dst, kp_ss.at[which], kp_rs.at[which], after, d)

    loaded(q, 0)
    send_query(0).start()
    loaded(k, 1)
    loaded(v, 2)
    send_keys(0).start()
    send_keys(1).start()

    def local_head(h):
        for half in (0, 1):
            rows, keys = pl.ds(256 * half, 256), 256 * (half + 1)
            t = dot_t(q[h, rows, :], k[h, 0:keys, :]) * BYTE_SCALE
            t = jnp.where(iota((256, keys), 1) <= iota((256, keys), 0) + 256 * half, t, NEG)
            peak = jnp.max(t, axis=1, keepdims=True)
            e = jnp.exp2(t - peak)
            total = jnp.sum(e, axis=1, keepdims=True)
            o_own[h, rows, :] = dot(e.astype(BF16), v[h, 0:keys, :]) * (1.0 / total)
            s_own[h, :, rows] = as_row(peak + jnp.log(total) * LOG2E)

    def cross_half(half, queries, keys, values, o_dst, s_dst):
        rows, n = pl.ds(256 * half, 256), 512 - 256 * half
        t = dot_t(queries[rows, :], keys[256 * half : 512, :]) * BYTE_SCALE
        t = jnp.where(iota((256, n), 1) > iota((256, n), 0), t, NEG)
        peak = jnp.max(t, axis=1, keepdims=True)
        e = jnp.exp2(t - peak)
        total = jnp.sum(e, axis=1, keepdims=True)
        o = dot(e.astype(BF16), values[256 * half : 512, :]) * (1.0 / total)
        o_dst[rows, :] = o.astype(BF16)
        lse = peak + jnp.log(total) * LOG2E
        if half == 1:
            lse = jnp.where(iota((256, 1), 0) == 255, NEG, lse)
        s_dst[:, rows] = as_row(lse)

    def remote_half(h, half):
        cross_half(half, q_next.at[h], k.at[h], v.at[h], o_send.at[h], s_send.at[h])

    def last_head():
        send_keys(0).wait_recv()
        send_keys(1).wait_recv()
        for half in (0, 1):
            cross_half(half, q.at[7], k_prev, v_prev, o_recv.at[7], s_recv.at[7])

    def send_out(h, half):
        rows = pl.ds(256 * half, 256)
        return remote(o_send.at[h, rows], o_recv.at[h, rows], o_ss.at[0], o_rs.at[h], after, d)

    def whole_out(h):
        return remote(o_send.at[h], o_recv.at[h], o_ss.at[0], o_rs.at[h], after, d)

    def send_stat(h):
        return remote(s_send.at[h], s_recv.at[h], s_ss.at[0], s_rs.at[h], after, d)

    stages = {
        0: [(from_z, 1)],
        1: [(from_x, 0)],
        2: [(from_z, 2)],
        4: [(from_z, 3), (from_x, 7)],
        5: [(from_x, 1)],
        6: [(from_z, 4), (from_far, 0)],
        7: [(from_x, 6), (last_head,)],
        8: [(from_x, 2)],
        9: [(from_far, 7)],
        10: [(from_x, 5), (from_far, 1)],
        11: [(from_x, 3), (from_x, 4)],
        12: [(from_far, 6)],
        13: [(from_far, 2)],
    }

    def forward(stage):
        for step, *i in stage:
            step(*i)

    @pl.loop(0, 4)
    def _(h):
        local_head(h)

        @pl.when(h < 3)
        def _():
            send_query(h + 1).start()

    weights_z()

    p80, n80 = iota((80, 640), 0), iota((80, 640), 1)
    repeat = n80 == p80
    for i in range(1, 8):
        repeat = repeat | (n80 == p80 + 80 * i)
    of_row = iota((8, 640), 1) - 80 * iota((8, 640), 0)
    of_row = (of_row >= 0) & (of_row < 80)
    for c in range(4):
        live = (starts[8 * c : 8 * c + 8, :] < 512).astype(BF16)
        spread_out = dot(live, repeat.astype(BF16))
        live_bias[c] = jnp.sum(jnp.where(of_row, (spread_out - 1.0) * -NEG, 0.0), axis=0, keepdims=True)

    @pl.loop(0, 7)
    def _(h):
        for half in (0, 1):
            unit = 2 * h + half
            send_query(unit).wait_recv()

            @pl.when(unit < 14 - IN_FLIGHT)
            def _():
                send_query(unit + IN_FLIGHT).start()

            remote_half(h, half)
            send_out(h, half).start()
            if half == 1:
                send_stat(h).start()

            @pl.when(h < 2)
            def _():
                local_head(4 + unit)

            for at, stage in stages.items():
                if at % 2 == half:
                    pl.when(h == at // 2)(functools.partial(forward, stage))

    for i in (5, 3, 4):
        from_far(i)

    def merge(h, squares):
        @pl.when(h < 7)
        def _():
            whole_out(h).wait_recv()
            send_stat(h).wait_recv()

        own = s_own[h]
        other = jnp.where(s == 0, NEG, s_recv[h])
        peak = jnp.maximum(own, other)
        a, b = jnp.exp2(own - peak), jnp.exp2(other - peak)
        share = jnp.transpose(jnp.broadcast_to(b / (a + b), (128, 512)))
        mine = o_own[h]
        mix = mine + share * (o_recv[h].astype(F32) - mine)
        o_own[h] = mix
        return squares + mix * mix

    squares = lax.fori_loop(0, 8, merge, jnp.zeros((512, 128), F32))
    scale = lax.rsqrt(jnp.sum(squares, axis=1, keepdims=True) * (1.0 / 1024) + EPS)
    for h in range(8):
        enc[h] = (o_own[h] * scale * gain_row(byte_gain, h, 128)).astype(BF16)
    enc_out = pltpu.make_async_copy(enc, enc_hbm, out_sem.at[0])
    enc_out.start()

    row = jnp.broadcast_to(starts[pl.ds(s, 1), :].astype(F32), (80, 80))
    r80, c80 = iota((80, 80), 0), iota((80, 80), 1)
    first = jnp.sum(jnp.where(c80 == r80, row, 0.0), axis=1, keepdims=True)
    stop = jnp.sum(jnp.where(c80 == r80 + 1, row, 0.0), axis=1, keepdims=True)
    stop = jnp.where(iota((80, 1), 0) == 79, 512.0, stop)
    at = iota((80, 512), 1).astype(F32)
    member = (at >= first) & (at < stop)
    for h in range(8):
        score = dot_t(pool_query[...], enc[h])[h : h + 1, :] * BYTE_SCALE
        t = jnp.where(member, score, NEG)
        peak = jnp.max(t, axis=1, keepdims=True)
        e = jnp.exp2(t - peak)
        total = jnp.sum(e, axis=1, keepdims=True)
        weights = (e * jnp.where(first < 512.0, 1.0 / total, 0.0)).astype(BF16)
        pooled[:, 128 * h : 128 * h + 128] = dot(weights, enc[h]).astype(BF16)

    half_of_w = w.at[0:4]
    remote(half_of_w, half_of_w, wc_ss.at[0], wc_rs.at[0], s, partner).wait_recv()

    def lift(p, squares):
        left = w[p, :, 0:32, :].reshape(1024, 128)
        right = w[p, :, 32:64, :].reshape(1024, 128)
        got = dot(pooled[...], jnp.concatenate([left, right], axis=1))
        lifted[p] = got
        return squares + got * got

    squares = lax.fori_loop(0, 8, lift, jnp.zeros((80, 256), F32))
    scale = lax.rsqrt(jnp.sum(squares, axis=1, keepdims=True) * (1.0 / 2048) + EPS)
    for p in range(8):
        got = (lifted[p] * scale * gain_row(patch_gain, p, 256)).astype(BF16)
        x_q[p] = got
        patch_in[:, 256 * p : 256 * p + 256] = got
    low = iota((80, 128), 1) < 64

    @pl.loop(0, 4)
    def _(p):
        keys = w[p, :, 64:128, :].reshape(2048, 128)
        values = w[p + 4, :, 64:128, :].reshape(2048, 128)
        got = dot(patch_in[...], jnp.concatenate([keys, values], axis=1))
        key, value = got[:, 0:128], got[:, 128:256]
        x_kv[2 * p] = jnp.where(low, key, pltpu.roll(value, 64, 1)).astype(BF16)
        x_kv[2 * p + 1] = jnp.where(low, pltpu.roll(key, 64, 1), value).astype(BF16)

    def kv_to(i):
        to = lax.rem(z + i, 8)
        return remote(x_kv.at[to], kv_all.at[z, yh], kz_ss.at[0], kz_rs.at[i - 1], along_z(i), d)

    def q_to(i):
        to = lax.rem(z + i, 8)
        return remote(x_q.at[to], q_all.at[z], qz_ss.at[0], qz_rs.at[i - 1], along_z(i), d)

    def kv_from(slot):
        i = lax.rem(z - slot + 7, 8)
        dst = kv_all.at[slot, yh]
        return remote(dst, dst, kz_ss.at[0], kz_rs.at[i], s, partner)

    def q_from(slot):
        i = lax.rem(z - slot + 7, 8)
        dst = q_all.at[slot]
        return remote(dst, dst, qz_ss.at[0], qz_rs.at[i], s, partner)

    for i in FAR_FIRST:
        kv_to(i).start()

    def send_queries():
        for i in FAR_FIRST:
            q_to(i).start()

    pl.when(z < 4)(send_queries)
    kv_all[z, yh] = x_kv[z]
    q_all[z] = x_q[z]

    sent(q.at[0:7], q_ss)
    sent(o_send.at[0:7], o_ss)
    sent(s_send.at[0:7], s_ss)
    send_keys(0).wait_send()
    send_keys(1).wait_send()
    sent(w.at[0, 0:3], wy_ss)
    sent(w.at[0, 0:16], zu_ss)
    sent(w.at[0, 0:12], zd_ss)
    sent(w.at[0], wp_ss)
    sent(w.at[0], wm_ss)
    sent(w.at[0], w2_ss)
    sent(half_of_w, wc_ss)

    y_up, y_down = lax.rem(yh + 1, 4), lax.rem(yh + 3, 4)

    def kv_up(slot, whose):
        ours = kv_all.at[slot, whose]
        return remote(ours, ours, yp_ss.at[0], yp_rs.at[slot], along_y(1), d)

    def kv_down(slot, whose):
        ours = kv_all.at[slot, whose]
        return remote(ours, ours, ym_ss.at[0], ym_rs.at[slot], along_y(3), d)

    def kv_far_up(slot, whose):
        ours = kv_all.at[slot, whose]
        return remote(ours, ours, yf_ss.at[0], yf_rs.at[slot], along_y(1), d)

    def kv_far_down(slot, whose):
        ours = kv_all.at[slot, whose]
        return remote(ours, ours, yf_ss.at[0], yf_rs.at[slot], along_y(3), d)

    def forward_kv(slot):
        @pl.when(slot != z)
        def _():
            kv_from(slot).wait_recv()

        kv_up(slot, yh).start()
        kv_down(slot, yh).start()

    def relay(slot):
        kv_up(slot, y_down).wait_recv()
        kv_down(slot, y_up).wait_recv()

        @pl.when(lax.rem(slot, 2) == 0)
        def _():
            kv_far_up(slot, y_down).start()

        @pl.when(lax.rem(slot, 2) == 1)
        def _():
            kv_far_down(slot, y_up).start()

    def out_to(to):
        return remote(o_out.at[to], o_in.at[z], oz_ss.at[0], oz_rs.at[z], to * 4 + yh, d)

    def out_from(slot):
        dst = o_in.at[slot]
        return remote(dst, dst, oz_ss.at[0], oz_rs.at[slot], s, partner)

    r320 = iota((320, 1), 0)
    r320 = jnp.where(r320 >= 240, r320 - 240, jnp.where(r320 >= 160, r320 - 160, jnp.where(r320 >= 80, r320 - 80, r320)))

    low_keys = iota((640, 128), 1) < 64

    def gathered_query(slot):
        @pl.when(slot != z)
        def _():
            q_from(slot).wait_recv()

        heads = []
        for tile in (0, 1):
            pair = q_all[slot, :, 128 * tile : 128 * tile + 128].astype(F32)
            heads += [jnp.where(low, pair, 0.0), jnp.where(low, pltpu.roll(pair, 64, 1), 0.0)]
        return jnp.concatenate(heads, axis=0).astype(BF16)

    def patch_pair(pair):
        slots = (2 * pair, 2 * pair + 1)
        queries = [gathered_query(slot) for slot in slots]

        def chunk(c, state, last):
            rows = kv_all[pl.ds(2 * c, 2)].reshape(640, 128)
            values = jnp.where(low_keys, jnp.ones((), BF16), rows)
            bias = live_bias[c]
            new = []
            for i in (0, 1):
                peak, acc = state[i]
                t = dot_t(queries[i], rows) * PATCH_SCALE + bias
                if last:
                    t = jnp.where(iota((320, 640), 1) <= i * 320 + yh * 80 + r320, t, NEG)
                peak_new = jnp.maximum(peak, jnp.max(t, axis=1, keepdims=True))
                e = jnp.exp2(t - peak_new).astype(BF16)
                new.append((peak_new, acc * jnp.exp2(peak - peak_new) + dot(e, values)))
            return tuple(new)

        start = (jnp.full((320, 1), NEG, F32), jnp.zeros((320, 128), F32))
        state = lax.fori_loop(0, pair, functools.partial(chunk, last=False), (start, start))
        state = chunk(pair, state, True)
        for slot, (_, acc) in zip(slots, state):
            out = acc * (1.0 / acc[:, 0:1])
            for tile in (0, 1):
                even, odd = out[160 * tile : 160 * tile + 80], out[160 * tile + 80 : 160 * tile + 160]
                o_out[slot, :, 128 * tile : 128 * tile + 128] = jnp.where(low, pltpu.roll(even, 64, 1), odd).astype(BF16)

            @pl.when(slot != z)
            def _():
                out_to(slot).start()

            @pl.when(slot == z)
            def _():
                o_in[slot] = o_out[slot]

    def far_arrival(slot):
        kv_far_up(slot, lax.rem(yh + 2, 4)).wait_recv()

    @pl.loop(0, 4)
    def _(slot):
        forward_kv(slot)

    pl.when(z >= 4)(send_queries)

    @pl.loop(0, 4)
    def _(pair):
        @pl.when(pair == 0)
        def _():
            relay(0)
            relay(1)
            forward_kv(4)
            forward_kv(5)

        @pl.when(pair == 1)
        def _():
            forward_kv(6)
            forward_kv(7)

        @pl.when(pair < 3)
        def _():
            relay(2 * pair + 2)
            relay(2 * pair + 3)

        far_arrival(2 * pair)
        far_arrival(2 * pair + 1)
        patch_pair(pair)

    def mixed_out(slot):
        return pltpu.make_async_copy(o_in.at[slot], mixed_hbm.at[slot], out_sem.at[1])

    @pl.loop(0, 8)
    def _(slot):
        @pl.when(slot != z)
        def _():
            out_from(slot).wait_recv()

        mixed_out(slot).start()

    sent(x_kv.at[0:7], kz_ss)
    sent(x_q.at[0:7], qz_ss)
    sent(x_kv, yp_ss)
    sent(x_kv, ym_ss)
    sent(x_kv, yf_ss)
    sent(o_out.at[0:7], oz_ss)
    enc_out.wait()
    pltpu.make_async_copy(o_in, mixed_hbm, out_sem.at[1]).wait()


def decode_kernel(
    enc_hbm, mixed_hbm, out_gain_hbm, dec_gain_hbm, starts_hbm, byte_out, patch_out,
    cross, enc, mixed, out_gain, dec_gain, starts, sem, enc_sem, small_sem,
):
    small = [
        pltpu.make_async_copy(src, dst, small_sem.at[i])
        for i, (src, dst) in enumerate(((out_gain_hbm, out_gain), (dec_gain_hbm, dec_gain), (starts_hbm, starts)))
    ]
    mixed_in = pltpu.make_async_copy(mixed_hbm, mixed, sem)
    mixed_in.start()

    for copy in small:
        copy.start()
    enc_in = pltpu.make_async_copy(enc_hbm, enc, enc_sem)
    enc_in.start()
    for copy in small:
        copy.wait()
    row = starts[pl.ds(lax.axis_index("seq"), 1), :]
    wide = jnp.broadcast_to(row.astype(F32), (80, 80))
    first = jnp.sum(jnp.where(iota((80, 80), 1) == iota((80, 80), 0), wide, 0.0), axis=1, keepdims=True)
    alive = (first < 512.0).astype(F32)
    mixed_in.wait()
    enc_in.wait()
    squares = jnp.zeros((80, 256), F32)
    for h in range(8):
        got = mixed[h].astype(F32)
        squares = squares + got * got
    scale = lax.rsqrt(jnp.sum(squares, axis=1, keepdims=True) * (1.0 / 2048) + EPS)
    allowed = row <= iota((512, 80), 0)
    squares = jnp.zeros((512, 128), F32)
    for h in range(8):
        patch = (mixed[h].astype(F32) * scale * gain_row(out_gain, h, 256) * alive).astype(BF16)
        patch_out[:, 256 * h : 256 * h + 256] = patch
        t = jnp.where(allowed, dot_t(enc[h], patch[:, 0:128]) * BYTE_SCALE, NEG)
        peak = jnp.max(t, axis=1, keepdims=True)
        e = jnp.exp2(t - peak)
        total = jnp.sum(e, axis=1, keepdims=True)
        got = dot(e.astype(BF16), patch[:, 128:256]) * (1.0 / total)
        cross[h] = got
        squares = squares + got * got
    scale = lax.rsqrt(jnp.sum(squares, axis=1, keepdims=True) * (1.0 / 1024) + EPS)
    for h in range(8):
        byte_out[:, 128 * h : 128 * h + 128] = (cross[h] * scale * gain_row(dec_gain, h, 128)).astype(BF16)


def per_device(
    byte_q, byte_k, byte_v, byte_gain, pool_query, w_up, patch_gain, w_kv, out_gain, dec_gain, patch_start
):
    hbm = pl.BlockSpec(memory_space=pl.ANY)
    vmem = pl.BlockSpec(memory_space=pltpu.VMEM)
    dma = pltpu.SemaphoreType.DMA
    enc, mixed = pl.pallas_call(
        main_kernel,
        out_shape=(
            jax.ShapeDtypeStruct((8, 512, 128), BF16),
            jax.ShapeDtypeStruct((8, 80, 256), BF16),
        ),
        in_specs=[hbm] * 5 + [vmem] * 4,
        out_specs=(hbm, hbm),
        scratch_shapes=[
            pltpu.VMEM((8, 512, 128), BF16),
            pltpu.VMEM((8, 512, 128), BF16),
            pltpu.VMEM((8, 512, 128), BF16),
            pltpu.VMEM((8, 512, 128), BF16),
            pltpu.VMEM((512, 128), BF16),
            pltpu.VMEM((512, 128), BF16),
            pltpu.VMEM((8, 512, 128), BF16),
            pltpu.VMEM((8, 512, 128), BF16),
            pltpu.VMEM((8, 1, 512), F32),
            pltpu.VMEM((8, 1, 512), F32),
            pltpu.VMEM((8, 512, 128), F32),
            pltpu.VMEM((8, 1, 512), F32),
            pltpu.VMEM((8, 512, 128), BF16),
            pltpu.VMEM((8, 32, 128, 128), BF16),
            pltpu.VMEM((80, 1024), BF16),
            pltpu.VMEM((8, 80, 256), F32),
            pltpu.VMEM((80, 2048), BF16),
            pltpu.VMEM((8, 80, 256), BF16),
            pltpu.VMEM((8, 80, 128), BF16),
            pltpu.VMEM((8, 4, 80, 128), BF16),
            pltpu.VMEM((8, 80, 256), BF16),
            pltpu.VMEM((8, 80, 256), BF16),
            pltpu.VMEM((8, 80, 256), BF16),
            pltpu.VMEM((4, 1, 640), F32),
            dma((4,)),
            dma((2,)),
            dma((2,)),
            dma((2,)),
            *[dma((1,)), dma((16,))],
            *[dma((1,)), dma((8,))] * 2,
            *[dma((1,)), dma((1,))],
            *[dma((1,)), dma((4,))],
            *[dma((1,)), dma((3,))],
            *[dma((1,)), dma((8,))] * 3,
            *[dma((1,)), dma((1,))],
            *[dma((1,)), dma((7,))] * 2,
            *[dma((1,)), dma((8,))] * 4,
        ],
        compiler_params=pltpu.CompilerParams(
            collective_id=0, has_side_effects=True, vmem_limit_bytes=60 * 1024 * 1024
        ),
    )(
        byte_q, byte_k, byte_v, w_up, w_kv,
        byte_gain, pool_query, patch_gain, patch_start,
    )
    return pl.pallas_call(
        decode_kernel,
        out_shape=(
            jax.ShapeDtypeStruct((512, 1024), BF16),
            jax.ShapeDtypeStruct((80, 2048), BF16),
        ),
        in_specs=[hbm] * 5,
        out_specs=(vmem, vmem),
        scratch_shapes=[
            pltpu.VMEM((8, 512, 128), F32),
            pltpu.VMEM((8, 512, 128), BF16),
            pltpu.VMEM((8, 80, 256), BF16),
            pltpu.VMEM((2048,), BF16),
            pltpu.VMEM((1024,), BF16),
            pltpu.VMEM((32, 80), jnp.int32),
            dma,
            dma,
            dma((3,)),
        ],
        compiler_params=pltpu.CompilerParams(vmem_limit_bytes=60 * 1024 * 1024),
    )(
        enc, mixed, out_gain, dec_gain, patch_start
    )


def solution(mesh):
    placed = (
        P(("doc", "seq"), None),
        P(("doc", "seq"), None),
        P(("doc", "seq"), None),
        P(),
        P(),
        P("seq", None),
        P(),
        P("seq", None),
        P(),
        P(),
        P("doc", None),
    )
    return jax.shard_map(
        per_device,
        mesh=mesh,
        in_specs=placed,
        out_specs=(P(("doc", "seq"), None), P(("doc", "seq"), None)),
        check_vma=False,
    )
```
